32 devices in a mesh: row: 4 (over y, x), bus: 8 (over z, core).
Axes of the slice: x: 2, y: 2, z: 4, core: 2. Of those that a mesh axis runs over, the one named last changes fastest.
Arguments:
- monitored: bfloat16 [512, 32768], P('row', 'bus'), may hold values from -6 to 6
- outaged: bfloat16 [256, 32768], P('row', 'bus'), may hold values from -6 to 6
- bus_weight: float32 [32768], P('bus'), may hold values from 0.5 to 4
- lodf_table: float32 [1024], replicated, may hold values from -1.5 to 1.5
- mon_id: int32 [2048], P('row'), may hold values from 0 to 511
- out_id: int32 [2048], P('row'), may hold values from 0 to 255
- lodf_idx: int32 [2048], P('row'), may hold values from 0 to 1023
Outputs:
- gram: float32 [2048, 2048], P('row', 'bus')
The draws below stay inside these ranges and needn't reach their ends.
All inputs are finite; a program needn't handle non-finite values.
Results may differ from the reference program's by a relative error of at most 0.0007.
Values may be sent and summed in bfloat16 or wider, within the bound.
A program may use at most 128 MiB of HBM per device.

```python
import math
import jax
import jax.numpy as jnp
import numpy as np

NB = 32768
NLODF = 1024
K = 2048
NMON = 512
NOUT = 256


def touch_ends(result, rng, smallest, largest):
    spot = [jax.random.randint(jax.random.fold_in(rng, axis), (), 0, length) for axis, length in enumerate(result.shape)]
    main_axis = result.shape.index(max(result.shape))
    next_to = spot[:main_axis] + [(spot[main_axis] + 1) % result.shape[main_axis]] + spot[main_axis + 1:]
    return result.at[tuple(spot)].set(smallest).at[tuple(next_to)].set(largest)


def level_of(stream_key, dims, pieces, least, high):
    def one(position, parts):
        steps = jax.random.uniform(jax.random.fold_in(jax.random.fold_in(stream_key, 6), position), (parts,), jnp.float32, least / len(pieces), high / len(pieces))
        return jnp.repeat(jnp.exp(steps), dims[position] // parts).reshape((-1,) + (1,) * (len(dims) - position - 1))

    gain = one(*pieces[0])
    for cut in pieces[1:]:
        gain = gain * one(*cut)
    return gain


def rank_table(number_of, lean):
    weights = [(1 << 20) // math.isqrt(rank ** lean) + 1 for rank in range(1, number_of + 1)]
    width = 1 + sum(weights) // (1 << 30)
    return np.cumsum(np.array([max(1, weight // width) for weight in weights]))


def skewed_ids(stream_key, dims, number_of, skew):
    listing = rank_table(number_of, skew)
    pick = jax.random.randint(jax.random.fold_in(stream_key, 1), dims, 0, int(listing[number_of - 1]))
    grade = jnp.searchsorted(jnp.asarray(listing, jnp.int32), pick, side="right")
    return jax.random.permutation(jax.random.fold_in(stream_key, 2), number_of)[grade].astype(jnp.int32)


def scatter_about(own_key, dims, scale, limit, split=(), dtype=jnp.bfloat16):
    result = scale * jax.random.normal(own_key, dims, jnp.float32)
    if split:
        result = result * level_of(own_key, dims, split, -0.22, 0.18)
    return jnp.clip(result, -limit, limit).astype(dtype)


def setup_inputs(seed: int = 0) -> dict:
    streams_of = jax.random.split(jax.random.key(seed), 8)
    monitored = scatter_about(streams_of[0], (NMON, NB), 1.0, 6.0, ((0, 4), (1, 8)))
    outaged = scatter_about(streams_of[1], (NOUT, NB), 1.0, 6.0, ((0, 4), (1, 8)))
    bus_weight = jnp.clip(jnp.exp(math.log(4.0) - 2.0794415 * jax.random.uniform(streams_of[2], (NB,), jnp.float32) ** level_of(streams_of[2], (NB,), ((0, 8),), -0.2, 0.2)), 0.5, 4.0)
    lodf_table = jnp.clip(jax.random.uniform(streams_of[3], (NLODF,), jnp.float32, -1.5, 1.5), -1.5, 1.5)
    mon_id = touch_ends(jax.random.randint(streams_of[4], (K,), 0, NMON), jax.random.fold_in(streams_of[4], 1), 0, NMON - 1).astype(jnp.int32)
    out_id = touch_ends(skewed_ids(streams_of[5], (K,), NOUT, 2), jax.random.fold_in(streams_of[5], 3), 0, NOUT - 1).astype(jnp.int32)
    lodf_idx = touch_ends(jax.random.randint(streams_of[6], (K,), 0, NLODF), jax.random.fold_in(streams_of[6], 1), 0, NLODF - 1).astype(jnp.int32)
    return dict(monitored=monitored, outaged=outaged, bus_weight=bus_weight, lodf_table=lodf_table, mon_id=mon_id, out_id=out_id, lodf_idx=lodf_idx)


def reference(monitored, outaged, bus_weight, lodf_table, mon_id, out_id, lodf_idx):
    coeff = jnp.take(lodf_table, lodf_idx, axis=0)
    base = jnp.take(monitored, mon_id, axis=0).astype(jnp.float32)
    extra = jnp.take(outaged, out_id, axis=0).astype(jnp.float32)
    post = (base + coeff[:, None] * extra).astype(jnp.bfloat16)
    weighted = (post.astype(jnp.float32) * (bus_weight / NB)[None, :]).astype(jnp.bfloat16)
    return jnp.dot(post, weighted.T, preferred_element_type=jnp.float32)
```

```python
import functools

import jax
import jax.numpy as jnp
from jax import lax
from jax.experimental import pallas as pl
from jax.experimental.pallas import tpu as pltpu
from jax.sharding import PartitionSpec as P

BLK = 256
F32 = jnp.float32
BF16 = jnp.bfloat16
MESH = pl.DeviceIdType.MESH


def split3(v):
    a = v.astype(BF16)
    rest = v - a.astype(F32)
    b = rest.astype(BF16)
    return a, b, (rest - b.astype(F32)).astype(BF16)


def dot(a, b):
    return jnp.dot(a, b, preferred_element_type=F32)


def dot_t(a, b):
    return lax.dot_general(a, b, (((1,), (1,)), ((), ())), preferred_element_type=F32)


def down(lanes):
    n = lanes.shape[1]
    return jnp.broadcast_to(lanes, (128, n)).T


def factors(idx, table_t, entries):
    n = idx.shape[1]
    parts = []
    for lo in range(0, n, 128):
        total = jnp.zeros((1, 128), F32)
        for e in range(0, entries, 128):
            rows = lax.broadcasted_iota(jnp.int32, (128, 128), 0) + e
            hit = jnp.where(rows == idx[:, lo:lo + 128], table_t[e:e + 128, :], 0.0)
            total = total + jnp.sum(hit, axis=0, keepdims=True)
        parts.append(total)
    return jnp.concatenate(parts, axis=1)


def kernel(dims, mon_ref, out_ref, w_ref, table_ref, mid_ref, oid_ref, lid_ref,
           gram_ref, x, xh, xl, gp, cbuf, gacc, rbuf, gs, zbuf, gz, full, tt, ids,
           brow, x_s, x_r, own, c_s, c_r, r_s, r_r, z_s, z_r, za_s, za_r, ra_s, ra_r, ca_s, ca_r):
    R, B, nb_all = dims
    Z = B // 2
    r = lax.axis_index("row")
    b = lax.axis_index("bus")
    core = lax.rem(b, 2)
    zi = lax.div(b, 2)
    mrows, cols = mon_ref.shape
    orows = out_ref.shape[0]
    nm, no = mrows * R, orows * R
    cq = cols // R
    nblk_m, nblk_o = nm // BLK, no // BLK
    nblk = nblk_m + nblk_o
    kl = mid_ref.shape[1]
    kc = kl * R // B
    H = gp.shape[0] // 2
    hq = H // R
    pz = hq // Z

    barrier = pltpu.get_barrier_semaphore()
    for d in range(1, R):
        pl.semaphore_signal(barrier, inc=1, device_id={"row": lax.rem(r + d, R)}, device_id_type=MESH)
    for d in range(1, Z):
        pl.semaphore_signal(barrier, inc=1, device_id={"bus": lax.rem(zi + d, Z) * 2 + core}, device_id_type=MESH)
    pl.semaphore_signal(barrier, inc=1, device_id={"bus": zi * 2 + (1 - core)}, device_id_type=MESH)
    pl.semaphore_wait(barrier, R - 1 + Z - 1 + 1)

    def quarter(ref, q):
        return ref.at[:, pl.ds(pl.multiple_of(q * cq, 128), cq)]

    mon_dst = x.at[pl.ds(pl.multiple_of(r * mrows, mrows), mrows), :]
    out_dst = x.at[pl.ds(pl.multiple_of(nm + r * orows, orows), orows), :]
    first = []
    for d in range(1, R):
        q = lax.rem(r + d, R)
        pairs = [(quarter(mon_ref, q), mon_dst), (quarter(out_ref, q), out_dst),
                 (mid_ref, ids.at[0, r]), (oid_ref, ids.at[1, r]), (lid_ref, ids.at[2, r])]
        for i, (src, dst) in enumerate(pairs):
            c = pltpu.make_async_remote_copy(
                src_ref=src, dst_ref=dst, send_sem=x_s.at[d - 1, i], recv_sem=x_r.at[d - 1, i],
                device_id={"row": q}, device_id_type=MESH)
            c.start()
            first.append(c)
    mine = [(quarter(mon_ref, r), mon_dst), (quarter(out_ref, r), out_dst),
            (mid_ref, ids.at[0, r]), (oid_ref, ids.at[1, r]), (lid_ref, ids.at[2, r])]
    local = []
    for i, (src, dst) in enumerate(mine):
        c = pltpu.make_async_copy(src, dst, own.at[i])
        c.start()
        local.append(c)

    entries = table_ref.shape[1]
    for e in range(0, entries, 128):
        tt[e:e + 128, :] = down(table_ref[:, e:e + 128])
    c_row = down(factors(lid_ref[...], tt, entries))
    lane = lax.broadcasted_iota(jnp.int32, (kl, 128), 1)
    mid_t = down(mid_ref[...].astype(F32)).astype(jnp.int32)
    for e in range(0, nm, 128):
        brow[:, e:e + 128] = jnp.where(mid_t == lane + e, 1.0, 0.0).astype(BF16)
    oid_t = down(oid_ref[...].astype(F32)).astype(jnp.int32)
    for e in range(0, no, 128):
        brow[:, nm + e:nm + e + 128] = jnp.where(oid_t == lane + e, 1.0, 0.0).astype(BF16)
    scale = w_ref[:, pl.ds(pl.multiple_of(r * cq, 128), cq)] * (1.0 / nb_all)

    for c in local:
        c.wait()
    for c in first:
        c.wait()

    for i in range(nblk):
        rows = slice(i * BLK, (i + 1) * BLK)
        v = x[rows, :].astype(F32) * scale
        h = v.astype(BF16)
        xh[rows, :] = h
        xl[rows, :] = (v - h.astype(F32)).astype(BF16)
    at = {}
    for i in range(nblk):
        for j in range(i, nblk):
            k = len(at)
            at[i, j] = k
            a = x[i * BLK:(i + 1) * BLK, :]
            rows = slice(j * BLK, (j + 1) * BLK)
            gp[k * BLK:(k + 1) * BLK, :] = dot_t(a, xh[rows, :]) + dot_t(a, xl[rows, :])
    if gp.shape[0] > len(at) * BLK:
        gp[len(at) * BLK:, :] = jnp.zeros((gp.shape[0] - len(at) * BLK, BLK), F32)

    other = zi * 2 + (1 - core)
    c = pltpu.make_async_remote_copy(
        src_ref=gp.at[pl.ds(pl.multiple_of((1 - core) * H, 8), H), :], dst_ref=cbuf,
        send_sem=c_s, recv_sem=c_r, device_id={"bus": other}, device_id_type=MESH)
    c.start()
    c.wait()
    gacc[...] = gp[pl.ds(pl.multiple_of(core * H, 8), H), :] + cbuf[...]

    copies = []
    for d in range(1, R):
        q = lax.rem(r + d, R)
        c = pltpu.make_async_remote_copy(
            src_ref=gacc.at[pl.ds(pl.multiple_of(q * hq, 8), hq), :], dst_ref=rbuf.at[d - 1],
            send_sem=r_s.at[d - 1], recv_sem=r_r.at[d - 1], device_id={"row": q}, device_id_type=MESH)
        c.start()
        copies.append(c)
    for c in copies:
        c.wait()
    total = gacc[pl.ds(pl.multiple_of(r * hq, 8), hq), :]
    for d in range(1, R):
        total = total + rbuf[d - 1]
    gs[...] = total

    copies = []
    for d in range(1, Z):
        q = lax.rem(zi + d, Z)
        c = pltpu.make_async_remote_copy(
            src_ref=gs.at[pl.ds(pl.multiple_of(q * pz, 8), pz), :], dst_ref=zbuf.at[d - 1],
            send_sem=z_s.at[d - 1], recv_sem=z_r.at[d - 1],
            device_id={"bus": q * 2 + core}, device_id_type=MESH)
        c.start()
        copies.append(c)
    for c in copies:
        c.wait()
    total = gs[pl.ds(pl.multiple_of(zi * pz, 8), pz), :]
    for d in range(1, Z):
        total = total + zbuf[d - 1]
    gz[...] = total

    start = core * H + r * hq
    piece = full.at[pl.ds(pl.multiple_of(start + zi * pz, 8), pz), :]
    keep = pltpu.make_async_copy(gz, piece, own.at[0])
    keep.start()
    copies = []
    for d in range(1, Z):
        c = pltpu.make_async_remote_copy(
            src_ref=gz, dst_ref=piece, send_sem=za_s.at[d - 1], recv_sem=za_r.at[d - 1],
            device_id={"bus": lax.rem(zi + d, Z) * 2 + core}, device_id_type=MESH)
        c.start()
        copies.append(c)
    keep.wait()
    for c in copies:
        c.wait()
    piece = full.at[pl.ds(pl.multiple_of(start, 8), hq), :]
    copies = []
    for d in range(1, R):
        c = pltpu.make_async_remote_copy(
            src_ref=piece, dst_ref=piece, send_sem=ra_s.at[d - 1], recv_sem=ra_r.at[d - 1],
            device_id={"row": lax.rem(r + d, R)}, device_id_type=MESH)
        c.start()
        copies.append(c)

    owner = lax.div(b * kc, kl)
    begin = pl.multiple_of(lax.rem(b * kc, kl), 128)
    mid_c = ids[0, owner, :, pl.ds(begin, kc)]
    oid_c = ids[1, owner, :, pl.ds(begin, kc)]
    c_col = factors(ids[2, owner, :, pl.ds(begin, kc)], tt, entries)
    sub = lax.broadcasted_iota(jnp.int32, (BLK, kc), 0)
    bcol = [jnp.where(sub + j * BLK == mid_c, 1.0, 0.0).astype(BF16) for j in range(nblk_m)]
    bcol += [jnp.where(sub + j * BLK == oid_c, 1.0, 0.0).astype(BF16) for j in range(nblk_o)]

    for c in copies:
        c.wait()
    piece = full.at[pl.ds(pl.multiple_of(core * H, 8), H), :]
    c = pltpu.make_async_remote_copy(
        src_ref=piece, dst_ref=piece, send_sem=ca_s, recv_sem=ca_r,
        device_id={"bus": other}, device_id_type=MESH)
    c.start()
    c.wait()

    t_m = [jnp.zeros((BLK, kc), F32) for _ in range(nblk)]
    t_o = [jnp.zeros((BLK, kc), F32) for _ in range(nblk)]
    for (i, j), k in at.items():
        g = full[k * BLK:(k + 1) * BLK, :]
        for to, frm, part in ((i, j, g), (j, i, g.T)) if i != j else ((i, j, g),):
            here = t_m if frm < nblk_m else t_o
            for p in split3(part):
                here[to] = here[to] + dot(p, bcol[frm])
    g_m = jnp.zeros((kl, kc), F32)
    g_o = jnp.zeros((kl, kc), F32)
    for i in range(nblk):
        s = brow[:, i * BLK:(i + 1) * BLK]
        acc = jnp.zeros((kl, kc), F32)
        for p in split3(t_m[i] + t_o[i] * c_col):
            acc = acc + dot(s, p)
        if i < nblk_m:
            g_m = g_m + acc
        else:
            g_o = g_o + acc
    gram_ref[...] = g_m + g_o * jnp.concatenate([c_row] * (kc // 128), axis=1)


def solution(mesh):
    R, B = mesh.shape["row"], mesh.shape["bus"]
    Z = B // 2

    def local(monitored, outaged, bus_weight, lodf_table, mon_id, out_id, lodf_idx):
        mrows, cols = monitored.shape
        orows = outaged.shape[0]
        n = (mrows + orows) * R
        cq = cols // R
        nblk = n // BLK
        kl = mon_id.shape[0]
        kc = kl * R // B
        unit = 8 * R * B
        packed = -(-(nblk * (nblk + 1) // 2 * BLK) // unit) * unit
        H = packed // 2
        hq = H // R
        pz = hq // Z
        vmem = pl.BlockSpec(memory_space=pltpu.VMEM)
        hbm = pl.BlockSpec(memory_space=pl.ANY)
        dma = pltpu.SemaphoreType.DMA
        return pl.pallas_call(
            functools.partial(kernel, (R, B, cols * B)),
            out_shape=jax.ShapeDtypeStruct((kl, kc), F32),
            in_specs=[hbm, hbm] + [vmem] * 5,
            out_specs=vmem,
            scratch_shapes=[
                pltpu.VMEM((n, cq), BF16),
                pltpu.VMEM((n, cq), BF16),
                pltpu.VMEM((n, cq), BF16),
                pltpu.VMEM((packed, BLK), F32),
                pltpu.VMEM((H, BLK), F32),
                pltpu.VMEM((H, BLK), F32),
                pltpu.VMEM((R - 1, hq, BLK), F32),
                pltpu.VMEM((hq, BLK), F32),
                pltpu.VMEM((Z - 1, pz, BLK), F32),
                pltpu.VMEM((pz, BLK), F32),
                pltpu.VMEM((packed, BLK), F32),
                pltpu.VMEM((lodf_table.shape[0], 128), F32),
                pltpu.VMEM((3, R, 1, kl), jnp.int32),
                pltpu.VMEM((kl, n), BF16),
                dma((R - 1, 5)), dma((R - 1, 5)), dma((5,)),
                dma, dma,
                dma((R - 1,)), dma((R - 1,)),
                dma((Z - 1,)), dma((Z - 1,)),
                dma((Z - 1,)), dma((Z - 1,)),
                dma((R - 1,)), dma((R - 1,)),
                dma, dma,
            ],
            compiler_params=pltpu.CompilerParams(
                collective_id=0, has_side_effects=True, vmem_limit_bytes=60 * 1024 * 1024),
        )(monitored, outaged, bus_weight[None, :], lodf_table[None, :],
          mon_id[None, :], out_id[None, :], lodf_idx[None, :])

    in_specs = (P("row", "bus"), P("row", "bus"), P("bus"), P(), P("row"), P("row"), P("row"))
    return jax.shard_map(local, mesh=mesh, in_specs=in_specs, out_specs=P("row", "bus"), check_vma=False)
```

```python
import functools

import jax
import jax.numpy as jnp
from jax import lax
from jax.experimental import pallas as pl
from jax.experimental.pallas import tpu as pltpu
from jax.sharding import PartitionSpec as P

BLK = 256
F32 = jnp.float32
BF16 = jnp.bfloat16
MESH = pl.DeviceIdType.MESH


def split3(v):
    a = v.astype(BF16)
    rest = v - a.astype(F32)
    b = rest.astype(BF16)
    return a, b, (rest - b.astype(F32)).astype(BF16)


def dot(a, b):
    return jnp.dot(a, b, preferred_element_type=F32)


def dot_t(a, b):
    return lax.dot_general(a, b, (((1,), (1,)), ((), ())), preferred_element_type=F32)


def down(lanes):
    n = lanes.shape[1]
    return jnp.broadcast_to(lanes, (128, n)).T


def factors(idx, table_t, entries):
    n = idx.shape[1]
    parts = []
    for lo in range(0, n, 128):
        total = jnp.zeros((1, 128), F32)
        for e in range(0, entries, 128):
            rows = lax.broadcasted_iota(jnp.int32, (128, 128), 0) + e
            hit = jnp.where(rows == idx[:, lo:lo + 128], table_t[e:e + 128, :], 0.0)
            total = total + jnp.sum(hit, axis=0, keepdims=True)
        parts.append(total)
    return jnp.concatenate(parts, axis=1)


class Stream:
    def __init__(self, refs, blocks, me, core, other, axes):
        (self.gp, self.cbuf, self.acc, self.b1, self.s1, self.b2, self.full,
         self.cs, self.cr, self.p1s, self.p1r, self.p2s, self.p2r,
         self.a1s, self.a1r, self.a2s, self.a2r, self.ds, self.dr) = refs
        self.blocks = blocks
        self.core, self.other = core, other
        (self.n1, self.i1, self.dev1), (self.n2, self.i2, self.dev2) = axes
        self.H = self.gp.shape[0] // 2
        self.h1 = self.H // self.n1
        self.pz = self.h1 // self.n2
        self.z_first = me

    def compute(self, x, xh, xl):
        for k, (i, j) in enumerate(self.blocks):
            left = x[i * BLK:(i + 1) * BLK, :]
            rows = slice(j * BLK, (j + 1) * BLK)
            self.gp[k * BLK:(k + 1) * BLK, :] = dot_t(left, xh[rows, :]) + dot_t(left, xl[rows, :])
        used = len(self.blocks) * BLK
        if self.gp.shape[0] > used:
            self.gp[used:, :] = jnp.zeros((self.gp.shape[0] - used, BLK), F32)

    def rows(self, start, count):
        return pl.ds(pl.multiple_of(start, 8), count)

    def send(self, src, dst, s, r, dev):
        c = pltpu.make_async_remote_copy(
            src_ref=src, dst_ref=dst, send_sem=s, recv_sem=r, device_id=dev, device_id_type=MESH)
        c.start()
        return c

    def pair_start(self):
        self.c = [self.send(self.gp.at[self.rows((1 - self.core) * self.H, self.H), :], self.cbuf,
                            self.cs, self.cr, self.other)]

    def wait(self):
        for c in self.c:
            c.wait()

    def one_start(self):
        self.wait()
        self.acc[...] = self.gp[self.rows(self.core * self.H, self.H), :] + self.cbuf[...]
        self.c = []
        for d in range(1, self.n1):
            q = lax.rem(self.i1 + d, self.n1)
            self.c.append(self.send(self.acc.at[self.rows(q * self.h1, self.h1), :], self.b1.at[d - 1],
                                    self.p1s.at[d - 1], self.p1r.at[d - 1], self.dev1(q)))

    def two_start(self):
        self.wait()
        total = self.acc[self.rows(self.i1 * self.h1, self.h1), :]
        for d in range(1, self.n1):
            total = total + self.b1[d - 1]
        self.s1[...] = total
        self.c = []
        for d in range(1, self.n2):
            q = lax.rem(self.i2 + d, self.n2)
            self.c.append(self.send(self.s1.at[self.rows(q * self.pz, self.pz), :], self.b2.at[d - 1],
                                    self.p2s.at[d - 1], self.p2r.at[d - 1], self.dev2(q)))

    def piece(self, z, r):
        i1, i2 = (z, r) if self.z_first else (r, z)
        return self.rows(self.core * self.H + i1 * self.h1 + i2 * self.pz, self.pz)

    def back_start(self):
        self.wait()
        total = self.s1[self.rows(self.i2 * self.pz, self.pz), :]
        for d in range(1, self.n2):
            total = total + self.b2[d - 1]
        if self.z_first:
            self.Z, self.zi, self.zdev = self.n1, self.i1, self.dev1
            self.R, self.r, self.rdev = self.n2, self.i2, self.dev2
        else:
            self.Z, self.zi, self.zdev = self.n2, self.i2, self.dev2
            self.R, self.r, self.rdev = self.n1, self.i1, self.dev1
        at = self.piece(self.zi, self.r)
        self.full[at, :] = total
        ref = self.full.at[at, :]
        self.zc = []
        for d in range(1, self.Z):
            self.zc.append(self.send(ref, ref, self.a1s.at[d - 1], self.a1r.at[d - 1],
                                     self.zdev(lax.rem(self.zi + d, self.Z))))
        self.c = []
        self.spread(0)

    def spread(self, e):
        ref = self.full.at[self.piece(lax.rem(self.zi + self.Z - e, self.Z), self.r), :]
        for d in range(1, self.R):
            self.c.append(self.send(ref, ref, self.a2s.at[e, d - 1], self.a2r.at[e, d - 1],
                                    self.rdev(lax.rem(self.r + d, self.R))))

    def spread_rest(self):
        for e in range(1, self.Z):
            self.zc[e - 1].wait()
            self.spread(e)

    def pair_back(self):
        self.wait()
        ref = self.full.at[self.rows(self.core * self.H, self.H), :]
        self.c = [self.send(ref, ref, self.ds, self.dr, self.other)]


def select(ids, block, rows_each, dev_rows, axis, shape):
    p = lax.broadcasted_iota(jnp.int32, shape, axis)
    if axis == 1:
        p = p + block[1]
    shift = rows_each.bit_length() - 1
    line = lax.shift_right_logical(p, jnp.full(shape, shift, jnp.int32)) * (dev_rows - rows_each) + p
    return jnp.where(ids == line + block[0] * rows_each, 1.0, 0.0).astype(BF16)


def kernel(dims, mon_ref, out_ref, w_ref, table_ref, mid_ref, oid_ref, lid_ref,
           gram_ref, x, xh, xl, tt, ids, brow, x_s, x_r, i_s, i_r, own, own_i, *rest):
    R, B, nb_all = dims
    Z = B // 2
    r = lax.axis_index("row")
    b = lax.axis_index("bus")
    core = lax.rem(b, 2)
    zi = lax.div(b, 2)
    mrows, cols = mon_ref.shape
    orows = out_ref.shape[0]
    each = BLK // R
    cq = cols // R
    nblk_o, nblk_m = orows // each, mrows // each
    nblk = nblk_m + nblk_o
    kl = mid_ref.shape[1]
    kc = kl * R // B

    def row_dev(q):
        return {"row": q}

    def z_dev(q):
        return {"bus": q * 2 + core}

    pair_dev = {"bus": zi * 2 + (1 - core)}
    barrier = pltpu.get_barrier_semaphore()
    for d in range(1, R):
        pl.semaphore_signal(barrier, inc=1, device_id=row_dev(lax.rem(r + d, R)), device_id_type=MESH)
    for d in range(1, Z):
        pl.semaphore_signal(barrier, inc=1, device_id=z_dev(lax.rem(zi + d, Z)), device_id_type=MESH)
    pl.semaphore_signal(barrier, inc=1, device_id=pair_dev, device_id_type=MESH)
    pl.semaphore_wait(barrier, R - 1 + Z - 1 + 1)

    def source(k, q):
        ref, k = (out_ref, k) if k < nblk_o else (mon_ref, k - nblk_o)
        return ref.at[k * each:(k + 1) * each, pl.ds(pl.multiple_of(q * cq, 128), cq)]

    def target(k):
        return x.at[pl.ds(pl.multiple_of(k * BLK + r * each, each), each), :]

    chunks = []
    for k in range(nblk):
        chunk = []
        for d in range(1, R):
            q = lax.rem(r + d, R)
            c = pltpu.make_async_remote_copy(
                src_ref=source(k, q), dst_ref=target(k), send_sem=x_s.at[d - 1, k], recv_sem=x_r.at[d - 1, k],
                device_id=row_dev(q), device_id_type=MESH)
            c.start()
            chunk.append(c)
        c = pltpu.make_async_copy(source(k, r), target(k), own.at[k])
        c.start()
        chunk.append(c)
        chunks.append(chunk)
    id_copies = []
    for i, src in enumerate((mid_ref, oid_ref, lid_ref)):
        for d in range(1, R):
            c = pltpu.make_async_remote_copy(
                src_ref=src, dst_ref=ids.at[i, r], send_sem=i_s.at[i, d - 1], recv_sem=i_r.at[i, d - 1],
                device_id=row_dev(lax.rem(r + d, R)), device_id_type=MESH)
            c.start()
            id_copies.append(c)
        c = pltpu.make_async_copy(src, ids.at[i, r], own_i.at[i])
        c.start()
        id_copies.append(c)

    entries = table_ref.shape[1]
    for e in range(0, entries, 128):
        tt[e:e + 128, :] = down(table_ref[:, e:e + 128])
    c_row = down(factors(lid_ref[...], tt, entries))
    oid_t = down(oid_ref[...].astype(F32)).astype(jnp.int32)
    mid_t = down(mid_ref[...].astype(F32)).astype(jnp.int32)
    for k in range(nblk):
        for e in range(0, BLK, 128):
            at = slice(k * BLK + e, k * BLK + e + 128)
            if k < nblk_o:
                brow[:, at] = select(oid_t, (k, e), each, orows, 1, (kl, 128))
            else:
                brow[:, at] = select(mid_t, (k - nblk_o, e), each, mrows, 1, (kl, 128))
    scale = w_ref[:, pl.ds(pl.multiple_of(r * cq, 128), cq)] * (1.0 / nb_all)

    n = len(rest) // 2
    last = nblk - 1
    ab = Stream(rest[:n], [(i, j) for i in range(last) for j in range(i, last)], True, core, pair_dev,
                ((Z, zi, z_dev), (R, r, row_dev)))
    bb = Stream(rest[n:], [(i, last) for i in range(nblk)], False, core, pair_dev,
                ((R, r, row_dev), (Z, zi, z_dev)))

    def arrive(k):
        for c in chunks[k]:
            c.wait()
        rows = slice(k * BLK, (k + 1) * BLK)
        v = x[rows, :].astype(F32) * scale
        h = v.astype(BF16)
        xh[rows, :] = h
        xl[rows, :] = (v - h.astype(F32)).astype(BF16)

    for k in range(last):
        arrive(k)
    ab.compute(x, xh, xl)
    ab.pair_start()
    ab.one_start()
    arrive(last)
    bb.compute(x, xh, xl)
    bb.pair_start()
    bb.one_start()
    ab.two_start()
    bb.two_start()
    ab.back_start()
    bb.back_start()
    ab.spread_rest()

    for c in id_copies:
        c.wait()
    owner = lax.div(b * kc, kl)
    begin = pl.multiple_of(lax.rem(b * kc, kl), 128)
    mid_c = ids[0, owner, :, pl.ds(begin, kc)]
    oid_c = ids[1, owner, :, pl.ds(begin, kc)]
    c_col = factors(ids[2, owner, :, pl.ds(begin, kc)], tt, entries)
    bcol = [select(oid_c, (k, 0), each, orows, 0, (BLK, kc)) for k in range(nblk_o)]
    bcol += [select(mid_c, (k, 0), each, mrows, 0, (BLK, kc)) for k in range(nblk_m)]

    t_m = [jnp.zeros((BLK, kc), F32) for _ in range(nblk)]
    t_o = [jnp.zeros((BLK, kc), F32) for _ in range(nblk)]

    def gather(stream):
        stream.wait()
        for k, (i, j) in enumerate(stream.blocks):
            g = stream.full[k * BLK:(k + 1) * BLK, :]
            for to, frm, part in ((i, j, g), (j, i, g.T)) if i != j else ((i, j, g),):
                here = t_o if frm < nblk_o else t_m
                for p in split3(part):
                    here[to] = here[to] + dot(p, bcol[frm])

    bb.spread_rest()
    ab.pair_back()
    gather(ab)
    bb.pair_back()
    gather(bb)
    g_m = jnp.zeros((kl, kc), F32)
    g_o = jnp.zeros((kl, kc), F32)
    for i in range(nblk):
        s = brow[:, i * BLK:(i + 1) * BLK]
        acc = jnp.zeros((kl, kc), F32)
        for p in split3(t_m[i] + t_o[i] * c_col):
            acc = acc + dot(s, p)
        if i < nblk_o:
            g_o = g_o + acc
        else:
            g_m = g_m + acc
    gram_ref[...] = g_m + g_o * jnp.concatenate([c_row] * (kc // 128), axis=1)


def solution(mesh):
    R, B = mesh.shape["row"], mesh.shape["bus"]
    Z = B // 2

    def stream_scratch(blocks, n1, n2):
        unit = 8 * R * B
        packed = -(-(blocks * BLK) // unit) * unit
        H = packed // 2
        h1 = H // n1
        pz = h1 // n2
        dma = pltpu.SemaphoreType.DMA
        return [
            pltpu.VMEM((packed, BLK), F32),
            pltpu.VMEM((H, BLK), F32),
            pltpu.VMEM((H, BLK), F32),
            pltpu.VMEM((n1 - 1, h1, BLK), F32),
            pltpu.VMEM((h1, BLK), F32),
            pltpu.VMEM((n2 - 1, pz, BLK), F32),
            pltpu.VMEM((packed, BLK), F32),
            dma, dma,
            dma((n1 - 1,)), dma((n1 - 1,)),
            dma((n2 - 1,)), dma((n2 - 1,)),
            dma((Z - 1,)), dma((Z - 1,)),
            dma((Z, R - 1)), dma((Z, R - 1)),
            dma, dma,
        ]

    def local(monitored, outaged, bus_weight, lodf_table, mon_id, out_id, lodf_idx):
        mrows, cols = monitored.shape
        orows = outaged.shape[0]
        n = (mrows + orows) * R
        cq = cols // R
        nblk = n // BLK
        kl = mon_id.shape[0]
        kc = kl * R // B
        vmem = pl.BlockSpec(memory_space=pltpu.VMEM)
        hbm = pl.BlockSpec(memory_space=pl.ANY)
        dma = pltpu.SemaphoreType.DMA
        return pl.pallas_call(
            functools.partial(kernel, (R, B, cols * B)),
            out_shape=jax.ShapeDtypeStruct((kl, kc), F32),
            in_specs=[hbm, hbm] + [vmem] * 5,
            out_specs=vmem,
            scratch_shapes=[
                pltpu.VMEM((n, cq), BF16),
                pltpu.VMEM((n, cq), BF16),
                pltpu.VMEM((n, cq), BF16),
                pltpu.VMEM((lodf_table.shape[0], 128), F32),
                pltpu.VMEM((3, R, 1, kl), jnp.int32),
                pltpu.VMEM((kl, n), BF16),
                dma((R - 1, nblk)), dma((R - 1, nblk)),
                dma((3, R - 1)), dma((3, R - 1)),
                dma((nblk,)), dma((3,)),
            ] + stream_scratch(nblk * (nblk - 1) // 2, Z, R) + stream_scratch(nblk, R, Z),
            compiler_params=pltpu.CompilerParams(
                collective_id=0, has_side_effects=True, vmem_limit_bytes=60 * 1024 * 1024),
        )(monitored, outaged, bus_weight[None, :], lodf_table[None, :],
          mon_id[None, :], out_id[None, :], lodf_idx[None, :])

    in_specs = (P("row", "bus"), P("row", "bus"), P("bus"), P(), P("row"), P("row"), P("row"))
    return jax.shard_map(local, mesh=mesh, in_specs=in_specs, out_specs=P("row", "bus"), check_vma=False)
```

```python
import functools

import jax
import jax.numpy as jnp
from jax import lax
from jax.experimental import pallas as pl
from jax.experimental.pallas import tpu as pltpu
from jax.sharding import PartitionSpec as P

BLK = 128
F32 = jnp.float32
BF16 = jnp.bfloat16
MESH = pl.DeviceIdType.MESH


def split3(v):
    a = v.astype(BF16)
    rest = v - a.astype(F32)
    b = rest.astype(BF16)
    return a, b, (rest - b.astype(F32)).astype(BF16)


def dot(a, b):
    return jnp.dot(a, b, preferred_element_type=F32)


def dot_t(a, b):
    return lax.dot_general(a, b, (((1,), (1,)), ((), ())), preferred_element_type=F32)


def down(lanes):
    n = lanes.shape[1]
    return jnp.broadcast_to(lanes, (128, n)).T


def factors(idx, table_t, entries):
    n = idx.shape[1]
    parts = []
    for lo in range(0, n, 128):
        total = jnp.zeros((1, 128), F32)
        for e in range(0, entries, 128):
            rows = lax.broadcasted_iota(jnp.int32, (128, 128), 0) + e
            hit = jnp.where(rows == idx[:, lo:lo + 128], table_t[e:e + 128, :], 0.0)
            total = total + jnp.sum(hit, axis=0, keepdims=True)
        parts.append(total)
    return jnp.concatenate(parts, axis=1)


class Stream:
    def __init__(self, refs, blocks, me, core, other, axes):
        (self.gp, self.cbuf, self.acc, self.b1, self.s1, self.b2, self.full,
         self.cs, self.cr, self.p1s, self.p1r, self.p2s, self.p2r,
         self.a1s, self.a1r, self.a2s, self.a2r, self.ds, self.dr) = refs
        self.blocks = blocks
        self.core, self.other = core, other
        (self.n1, self.i1, self.dev1), (self.n2, self.i2, self.dev2) = axes
        self.H = self.gp.shape[0] // 2
        self.h1 = self.H // self.n1
        self.pz = self.h1 // self.n2
        self.z_first = me

    def compute(self, x, xw):
        at = 0
        for k in self.blocks:
            m = (k + 1) * BLK
            both = dot_t(x[:m, :], xw[k])
            self.gp[at:at + m, :] = both[:, :BLK] + both[:, BLK:]
            at += m
        if self.gp.shape[0] > at:
            self.gp[at:, :] = jnp.zeros((self.gp.shape[0] - at, BLK), F32)

    def rows(self, start, count):
        return pl.ds(pl.multiple_of(start, 8), count)

    def send(self, src, dst, s, r, dev):
        c = pltpu.make_async_remote_copy(
            src_ref=src, dst_ref=dst, send_sem=s, recv_sem=r, device_id=dev, device_id_type=MESH)
        c.start()
        return c

    def pair_start(self):
        self.c = [self.send(self.gp.at[self.rows((1 - self.core) * self.H, self.H), :], self.cbuf,
                            self.cs, self.cr, self.other)]

    def wait(self):
        for c in self.c:
            c.wait()

    def one_start(self):
        self.wait()
        self.acc[...] = self.gp[self.rows(self.core * self.H, self.H), :] + self.cbuf[...]
        self.c = []
        for d in range(1, self.n1):
            q = lax.rem(self.i1 + d, self.n1)
            self.c.append(self.send(self.acc.at[self.rows(q * self.h1, self.h1), :], self.b1.at[d - 1],
                                    self.p1s.at[d - 1], self.p1r.at[d - 1], self.dev1(q)))

    def two_start(self):
        self.wait()
        total = self.acc[self.rows(self.i1 * self.h1, self.h1), :]
        for d in range(1, self.n1):
            total = total + self.b1[d - 1]
        self.s1[...] = total
        self.c = []
        for d in range(1, self.n2):
            q = lax.rem(self.i2 + d, self.n2)
            self.c.append(self.send(self.s1.at[self.rows(q * self.pz, self.pz), :], self.b2.at[d - 1],
                                    self.p2s.at[d - 1], self.p2r.at[d - 1], self.dev2(q)))

    def piece(self, z, r):
        i1, i2 = (z, r) if self.z_first else (r, z)
        return self.rows(self.core * self.H + i1 * self.h1 + i2 * self.pz, self.pz)

    def back_start(self):
        self.wait()
        total = self.s1[self.rows(self.i2 * self.pz, self.pz), :]
        for d in range(1, self.n2):
            total = total + self.b2[d - 1]
        if self.z_first:
            self.Z, self.zi, self.zdev = self.n1, self.i1, self.dev1
            self.R, self.r, self.rdev = self.n2, self.i2, self.dev2
        else:
            self.Z, self.zi, self.zdev = self.n2, self.i2, self.dev2
            self.R, self.r, self.rdev = self.n1, self.i1, self.dev1
        at = self.piece(self.zi, self.r)
        self.full[at, :] = total
        ref = self.full.at[at, :]
        self.zc = []
        for d in range(1, self.Z):
            self.zc.append(self.send(ref, ref, self.a1s.at[d - 1], self.a1r.at[d - 1],
                                     self.zdev(lax.rem(self.zi + d, self.Z))))
        self.c = []
        self.spread(0)

    def spread(self, e):
        ref = self.full.at[self.piece(lax.rem(self.zi + self.Z - e, self.Z), self.r), :]
        for d in range(1, self.R):
            self.c.append(self.send(ref, ref, self.a2s.at[e, d - 1], self.a2r.at[e, d - 1],
                                    self.rdev(lax.rem(self.r + d, self.R))))

    def spread_rest(self):
        for e in range(1, self.Z):
            self.zc[e - 1].wait()
            self.spread(e)

    def pair_back(self):
        self.wait()
        ref = self.full.at[self.rows(self.core * self.H, self.H), :]
        self.c = [self.send(ref, ref, self.ds, self.dr, self.other)]


def select(ids, block, rows_each, dev_rows, axis, shape):
    p = lax.broadcasted_iota(jnp.int32, shape, axis)
    if axis == 1:
        p = p + block[1]
    shift = rows_each.bit_length() - 1
    line = lax.shift_right_logical(p, jnp.full(shape, shift, jnp.int32)) * (dev_rows - rows_each) + p
    return jnp.where(ids == line + block[0] * rows_each, 1.0, 0.0).astype(BF16)


def kernel(dims, mon_ref, out_ref, w_ref, table_ref, mid_ref, oid_ref, lid_ref,
           gram_ref, x, xw, tt, ids, brow, t_o, t_m, x_s, x_r, i_s, i_r, own, own_i, *rest):
    R, B, nb_all = dims
    Z = B // 2
    r = lax.axis_index("row")
    b = lax.axis_index("bus")
    core = lax.rem(b, 2)
    zi = lax.div(b, 2)
    mrows, cols = mon_ref.shape
    orows = out_ref.shape[0]
    each = BLK // R
    cq = cols // R
    nblk_o, nblk_m = orows // each, mrows // each
    nblk = nblk_m + nblk_o
    kl = mid_ref.shape[1]
    kc = kl * R // B

    def row_dev(q):
        return {"row": q}

    def z_dev(q):
        return {"bus": q * 2 + core}

    pair_dev = {"bus": zi * 2 + (1 - core)}
    barrier = pltpu.get_barrier_semaphore()
    for d in range(1, R):
        pl.semaphore_signal(barrier, inc=1, device_id=row_dev(lax.rem(r + d, R)), device_id_type=MESH)
    for d in range(1, Z):
        pl.semaphore_signal(barrier, inc=1, device_id=z_dev(lax.rem(zi + d, Z)), device_id_type=MESH)
    pl.semaphore_signal(barrier, inc=1, device_id=pair_dev, device_id_type=MESH)
    pl.semaphore_wait(barrier, R - 1 + Z - 1 + 1)

    def source(k, q):
        ref, k = (out_ref, k) if k < nblk_o else (mon_ref, k - nblk_o)
        return ref.at[k * each:(k + 1) * each, pl.ds(pl.multiple_of(q * cq, 128), cq)]

    def target(k):
        return x.at[pl.ds(pl.multiple_of(k * BLK + r * each, each), each), :]

    chunks = []
    for k in range(nblk):
        chunk = []
        for d in range(1, R):
            q = lax.rem(r + d, R)
            c = pltpu.make_async_remote_copy(
                src_ref=source(k, q), dst_ref=target(k), send_sem=x_s.at[d - 1, k], recv_sem=x_r.at[d - 1, k],
                device_id=row_dev(q), device_id_type=MESH)
            c.start()
            chunk.append(c)
        c = pltpu.make_async_copy(source(k, r), target(k), own.at[k])
        c.start()
        chunk.append(c)
        chunks.append(chunk)
    id_copies = []
    for i, src in enumerate((mid_ref, oid_ref, lid_ref)):
        for d in range(1, R):
            c = pltpu.make_async_remote_copy(
                src_ref=src, dst_ref=ids.at[i, r], send_sem=i_s.at[i, d - 1], recv_sem=i_r.at[i, d - 1],
                device_id=row_dev(lax.rem(r + d, R)), device_id_type=MESH)
            c.start()
            id_copies.append(c)
        c = pltpu.make_async_copy(src, ids.at[i, r], own_i.at[i])
        c.start()
        id_copies.append(c)

    entries = table_ref.shape[1]
    for e in range(0, entries, 128):
        tt[e:e + 128, :] = down(table_ref[:, e:e + 128])
    c_row = down(factors(lid_ref[...], tt, entries))
    oid_t = down(oid_ref[...].astype(F32)).astype(jnp.int32)
    mid_t = down(mid_ref[...].astype(F32)).astype(jnp.int32)
    for k in range(nblk):
        for e in range(0, BLK, 128):
            at = slice(k * BLK + e, k * BLK + e + 128)
            if k < nblk_o:
                brow[:, at] = select(oid_t, (k, e), each, orows, 1, (kl, 128))
            else:
                brow[:, at] = select(mid_t, (k - nblk_o, e), each, mrows, 1, (kl, 128))
    scale = w_ref[:, pl.ds(pl.multiple_of(r * cq, 128), cq)] * (1.0 / nb_all)

    z_axis, row_axis = (Z, zi, z_dev), (R, r, row_dev)
    n = len(rest) // 3
    s1, s2, s3 = [
        Stream(rest[i * n:(i + 1) * n], blocks, z_first, core, pair_dev,
               (z_axis, row_axis) if z_first else (row_axis, z_axis))
        for i, (blocks, z_first) in enumerate(plan(nblk))]

    def arrive(k):
        for c in chunks[k]:
            c.wait()
        rows = slice(k * BLK, (k + 1) * BLK)
        v = x[rows, :].astype(F32) * scale
        h = v.astype(BF16)
        xw[k, :BLK, :] = h
        xw[k, BLK:, :] = (v - h.astype(F32)).astype(BF16)

    for stream in (s1, s2, s3):
        for k in stream.blocks:
            arrive(k)
        stream.compute(x, xw)
        stream.pair_start()
        stream.one_start()
    s1.two_start()
    s3.two_start()
    s2.two_start()
    s1.back_start()
    s3.back_start()
    s2.back_start()
    s1.spread_rest()

    for c in id_copies:
        c.wait()
    owner = lax.div(b * kc, kl)
    begin = pl.multiple_of(lax.rem(b * kc, kl), 128)
    mid_c = ids[0, owner, :, pl.ds(begin, kc)]
    oid_c = ids[1, owner, :, pl.ds(begin, kc)]
    c_col = factors(ids[2, owner, :, pl.ds(begin, kc)], tt, entries)
    bcol = [select(oid_c, (k, 0), each, orows, 0, (BLK, kc)) for k in range(nblk_o)]
    bcol += [select(mid_c, (k, 0), each, mrows, 0, (BLK, kc)) for k in range(nblk_m)]

    t_o[...] = jnp.zeros_like(t_o)
    t_m[...] = jnp.zeros_like(t_m)
    cut = nblk_o * BLK

    def times(v, cols_of):
        total = None
        for p in split3(v):
            total = dot(p, cols_of) if total is None else total + dot(p, cols_of)
        return total

    def gather(stream):
        stream.wait()
        at = 0
        for k in stream.blocks:
            m = (k + 1) * BLK
            strip = stream.full[at:at + m, :]
            at += m
            t = t_o if k < nblk_o else t_m
            t[:m, :] = t[:m, :] + times(strip, bcol[k])
            rows = slice(k * BLK, m)
            above = min(k * BLK, cut)
            if above > 0:
                part = jnp.concatenate(bcol[:above // BLK], axis=0)
                t_o[rows, :] = t_o[rows, :] + times(strip[:above, :].T, part)
            if k * BLK > cut:
                part = jnp.concatenate(bcol[nblk_o:k], axis=0)
                t_m[rows, :] = t_m[rows, :] + times(strip[cut:k * BLK, :].T, part)

    s1.pair_back()
    s3.spread_rest()
    s2.spread_rest()
    gather(s1)
    s3.pair_back()
    gather(s3)
    s2.pair_back()
    gather(s2)
    t = t_m[...] + t_o[...] * c_col
    g_o = times_left(brow[:, :cut], t[:cut, :])
    g_m = times_left(brow[:, cut:], t[cut:, :])
    gram_ref[...] = g_m + g_o * jnp.concatenate([c_row] * (kc // 128), axis=1)


def times_left(s, v):
    a, b, c = split3(v)
    return dot(s, a) + dot(s, b) + dot(s, c)


def plan(nblk):
    half = nblk // 2
    return ((range(half), True), (range(half, nblk - 1), True), (range(nblk - 1, nblk), False))


def solution(mesh):
    R, B = mesh.shape["row"], mesh.shape["bus"]
    Z = B // 2

    def stream_scratch(blocks, n1, n2):
        unit = 8 * R * B
        packed = -(-(blocks * BLK) // unit) * unit
        H = packed // 2
        h1 = H // n1
        pz = h1 // n2
        dma = pltpu.SemaphoreType.DMA
        return [
            pltpu.VMEM((packed, BLK), F32),
            pltpu.VMEM((H, BLK), F32),
            pltpu.VMEM((H, BLK), F32),
            pltpu.VMEM((n1 - 1, h1, BLK), F32),
            pltpu.VMEM((h1, BLK), F32),
            pltpu.VMEM((n2 - 1, pz, BLK), F32),
            pltpu.VMEM((packed, BLK), F32),
            dma, dma,
            dma((n1 - 1,)), dma((n1 - 1,)),
            dma((n2 - 1,)), dma((n2 - 1,)),
            dma((Z - 1,)), dma((Z - 1,)),
            dma((Z, R - 1)), dma((Z, R - 1)),
            dma, dma,
        ]

    def local(monitored, outaged, bus_weight, lodf_table, mon_id, out_id, lodf_idx):
        mrows, cols = monitored.shape
        orows = outaged.shape[0]
        n = (mrows + orows) * R
        cq = cols // R
        nblk = n // BLK
        kl = mon_id.shape[0]
        kc = kl * R // B
        vmem = pl.BlockSpec(memory_space=pltpu.VMEM)
        hbm = pl.BlockSpec(memory_space=pl.ANY)
        dma = pltpu.SemaphoreType.DMA
        return pl.pallas_call(
            functools.partial(kernel, (R, B, cols * B)),
            out_shape=jax.ShapeDtypeStruct((kl, kc), F32),
            in_specs=[hbm, hbm] + [vmem] * 5,
            out_specs=vmem,
            scratch_shapes=[
                pltpu.VMEM((n, cq), BF16),
                pltpu.VMEM((nblk, 2 * BLK, cq), BF16),
                pltpu.VMEM((lodf_table.shape[0], 128), F32),
                pltpu.VMEM((3, R, 1, kl), jnp.int32),
                pltpu.VMEM((kl, n), BF16),
                pltpu.VMEM((n, kc), F32),
                pltpu.VMEM((n, kc), F32),
                dma((R - 1, nblk)), dma((R - 1, nblk)),
                dma((3, R - 1)), dma((3, R - 1)),
                dma((nblk,)), dma((3,)),
            ] + [
                ref for blocks, z_first in plan(nblk)
                for ref in stream_scratch(sum(k + 1 for k in blocks), *((Z, R) if z_first else (R, Z)))
            ],
            compiler_params=pltpu.CompilerParams(
                collective_id=0, has_side_effects=True, vmem_limit_bytes=60 * 1024 * 1024),
        )(monitored, outaged, bus_weight[None, :], lodf_table[None, :],
          mon_id[None, :], out_id[None, :], lodf_idx[None, :])

    in_specs = (P("row", "bus"), P("row", "bus"), P("bus"), P(), P("row"), P("row"), P("row"))
    return jax.shard_map(local, mesh=mesh, in_specs=in_specs, out_specs=P("row", "bus"), check_vma=False)
```

```python
import functools

import jax
import jax.numpy as jnp
from jax import lax
from jax.experimental import pallas as pl
from jax.experimental.pallas import tpu as pltpu
from jax.sharding import PartitionSpec as P

BLK = 128
F32 = jnp.float32
BF16 = jnp.bfloat16
MESH = pl.DeviceIdType.MESH


def split(v):
    a = v.astype(BF16)
    return a, (v - a.astype(F32)).astype(BF16)


def dot(a, b):
    return jnp.dot(a, b, preferred_element_type=F32)


def dot_t(a, b):
    return lax.dot_general(a, b, (((1,), (1,)), ((), ())), preferred_element_type=F32)


def down(lanes):
    n = lanes.shape[1]
    return jnp.broadcast_to(lanes, (128, n)).T


def factors(idx, table_t, entries):
    n = idx.shape[1]
    parts = []
    for lo in range(0, n, 128):
        total = jnp.zeros((1, 128), F32)
        for e in range(0, entries, 128):
            rows = lax.broadcasted_iota(jnp.int32, (128, 128), 0) + e
            hit = jnp.where(rows == idx[:, lo:lo + 128], table_t[e:e + 128, :], 0.0)
            total = total + jnp.sum(hit, axis=0, keepdims=True)
        parts.append(total)
    return jnp.concatenate(parts, axis=1)


class Stream:
    def __init__(self, refs, blocks, me, core, other, axes):
        (self.gp, self.cbuf, self.acc, self.b1, self.s1, self.b2, self.full,
         self.cs, self.cr, self.p1s, self.p1r, self.p2s, self.p2r,
         self.a1s, self.a1r, self.a2s, self.a2r, self.ds, self.dr) = refs
        self.blocks = blocks
        self.core, self.other = core, other
        (self.n1, self.i1, self.dev1), (self.n2, self.i2, self.dev2) = axes
        self.H = self.gp.shape[0] // 2
        self.h1 = self.H // self.n1
        self.pz = self.h1 // self.n2
        self.z_first = me

    def compute(self, x, xw):
        at = 0
        for k in self.blocks:
            m = (k + 1) * BLK
            both = dot_t(x[:m, :], xw[k])
            self.gp[at:at + m, :] = both[:, :BLK] + both[:, BLK:]
            at += m
        if self.gp.shape[0] > at:
            self.gp[at:, :] = jnp.zeros((self.gp.shape[0] - at, BLK), F32)

    def rows(self, start, count):
        return pl.ds(pl.multiple_of(start, 8), count)

    def send(self, src, dst, s, r, dev):
        c = pltpu.make_async_remote_copy(
            src_ref=src, dst_ref=dst, send_sem=s, recv_sem=r, device_id=dev, device_id_type=MESH)
        c.start()
        return c

    def pair_start(self):
        self.c = [self.send(self.gp.at[self.rows((1 - self.core) * self.H, self.H), :], self.cbuf,
                            self.cs, self.cr, self.other)]

    def wait(self):
        for c in self.c:
            c.wait()

    def one_start(self):
        self.wait()
        self.acc[...] = self.gp[self.rows(self.core * self.H, self.H), :] + self.cbuf[...]
        self.c = []
        for d in range(1, self.n1):
            q = lax.rem(self.i1 + d, self.n1)
            self.c.append(self.send(self.acc.at[self.rows(q * self.h1, self.h1), :], self.b1.at[d - 1],
                                    self.p1s.at[d - 1], self.p1r.at[d - 1], self.dev1(q)))

    def two_start(self):
        self.wait()
        total = self.acc[self.rows(self.i1 * self.h1, self.h1), :]
        for d in range(1, self.n1):
            total = total + self.b1[d - 1]
        self.s1[...] = total
        self.c = []
        for d in range(1, self.n2):
            q = lax.rem(self.i2 + d, self.n2)
            self.c.append(self.send(self.s1.at[self.rows(q * self.pz, self.pz), :], self.b2.at[d - 1],
                                    self.p2s.at[d - 1], self.p2r.at[d - 1], self.dev2(q)))

    def piece(self, z, r):
        i1, i2 = (z, r) if self.z_first else (r, z)
        return self.rows(self.core * self.H + i1 * self.h1 + i2 * self.pz, self.pz)

    def back_start(self):
        self.wait()
        total = self.s1[self.rows(self.i2 * self.pz, self.pz), :]
        for d in range(1, self.n2):
            total = total + self.b2[d - 1]
        if self.z_first:
            self.Z, self.zi, self.zdev = self.n1, self.i1, self.dev1
            self.R, self.r, self.rdev = self.n2, self.i2, self.dev2
        else:
            self.Z, self.zi, self.zdev = self.n2, self.i2, self.dev2
            self.R, self.r, self.rdev = self.n1, self.i1, self.dev1
        at = self.piece(self.zi, self.r)
        self.full[at, :] = total
        ref = self.full.at[at, :]
        self.zc = []
        for d in range(1, self.Z):
            self.zc.append(self.send(ref, ref, self.a1s.at[d - 1], self.a1r.at[d - 1],
                                     self.zdev(lax.rem(self.zi + d, self.Z))))
        self.c = []
        self.spread(0)

    def spread(self, e):
        ref = self.full.at[self.piece(lax.rem(self.zi + self.Z - e, self.Z), self.r), :]
        for d in range(1, self.R):
            self.c.append(self.send(ref, ref, self.a2s.at[e, d - 1], self.a2r.at[e, d - 1],
                                    self.rdev(lax.rem(self.r + d, self.R))))

    def spread_rest(self):
        for e in range(1, self.Z):
            self.zc[e - 1].wait()
            self.spread(e)

    def pair_back(self):
        self.wait()
        ref = self.full.at[self.rows(self.core * self.H, self.H), :]
        self.c = [self.send(ref, ref, self.ds, self.dr, self.other)]


def select(ids, block, rows_each, dev_rows, axis, shape):
    p = lax.broadcasted_iota(jnp.int32, shape, axis)
    if axis == 1:
        p = p + block[1]
    shift = rows_each.bit_length() - 1
    line = lax.shift_right_logical(p, jnp.full(shape, shift, jnp.int32)) * (dev_rows - rows_each) + p
    return jnp.where(ids == line + block[0] * rows_each, 1.0, 0.0).astype(BF16)


def kernel(dims, mon_ref, out_ref, w_hbm, table_hbm, mid_hbm, oid_hbm, lid_hbm,
           gram_ref, w_ref, table_ref, mid_ref, oid_ref, lid_ref, small, x, xw, tt, ids, brow, t_o, t_m, x_s, x_r, i_s, i_r, own, own_i, *rest):
    R, B, nb_all = dims
    Z = B // 2
    r = lax.axis_index("row")
    b = lax.axis_index("bus")
    core = lax.rem(b, 2)
    zi = lax.div(b, 2)
    mrows, cols = mon_ref.shape
    orows = out_ref.shape[0]
    each = BLK // R
    cq = cols // R
    nblk_o, nblk_m = orows // each, mrows // each
    nblk = nblk_m + nblk_o
    kl = mid_ref.shape[1]
    kc = kl * R // B
    loads = []
    for i, (src, dst) in enumerate(((w_hbm, w_ref), (table_hbm, table_ref), (mid_hbm, mid_ref),
                                    (oid_hbm, oid_ref), (lid_hbm, lid_ref))):
        c = pltpu.make_async_copy(src, dst, small.at[i])
        c.start()
        loads.append(c)

    def row_dev(q):
        return {"row": q}

    def z_dev(q):
        return {"bus": q * 2 + core}

    pair_dev = {"bus": zi * 2 + (1 - core)}
    barrier = pltpu.get_barrier_semaphore()
    for d in range(1, R):
        pl.semaphore_signal(barrier, inc=1, device_id=row_dev(lax.rem(r + d, R)), device_id_type=MESH)
    for d in range(1, Z):
        pl.semaphore_signal(barrier, inc=1, device_id=z_dev(lax.rem(zi + d, Z)), device_id_type=MESH)
    pl.semaphore_signal(barrier, inc=1, device_id=pair_dev, device_id_type=MESH)
    pl.semaphore_wait(barrier, R - 1 + Z - 1 + 1)

    def source(k, q):
        ref, k = (out_ref, k) if k < nblk_o else (mon_ref, k - nblk_o)
        return ref.at[k * each:(k + 1) * each, pl.ds(pl.multiple_of(q * cq, 128), cq)]

    def target(k):
        return x.at[pl.ds(pl.multiple_of(k * BLK + r * each, each), each), :]

    chunks = []
    for k in range(nblk):
        chunk = []
        for d in range(1, R):
            q = lax.rem(r + d, R)
            c = pltpu.make_async_remote_copy(
                src_ref=source(k, q), dst_ref=target(k), send_sem=x_s.at[d - 1, k], recv_sem=x_r.at[d - 1, k],
                device_id=row_dev(q), device_id_type=MESH)
            c.start()
            chunk.append(c)
        c = pltpu.make_async_copy(source(k, r), target(k), own.at[k])
        c.start()
        chunk.append(c)
        chunks.append(chunk)
    for c in loads:
        c.wait()
    id_copies = []
    for i, src in enumerate((mid_ref, oid_ref, lid_ref)):
        for d in range(1, R):
            c = pltpu.make_async_remote_copy(
                src_ref=src, dst_ref=ids.at[i, r], send_sem=i_s.at[i, d - 1], recv_sem=i_r.at[i, d - 1],
                device_id=row_dev(lax.rem(r + d, R)), device_id_type=MESH)
            c.start()
            id_copies.append(c)
        c = pltpu.make_async_copy(src, ids.at[i, r], own_i.at[i])
        c.start()
        id_copies.append(c)

    entries = table_ref.shape[1]
    for e in range(0, entries, 128):
        tt[e:e + 128, :] = down(table_ref[:, e:e + 128])
    c_row = down(factors(lid_ref[...], tt, entries))
    oid_t = down(oid_ref[...].astype(F32)).astype(jnp.int32)
    mid_t = down(mid_ref[...].astype(F32)).astype(jnp.int32)
    for k in range(nblk):
        for e in range(0, BLK, 128):
            at = slice(k * BLK + e, k * BLK + e + 128)
            if k < nblk_o:
                brow[:, at] = select(oid_t, (k, e), each, orows, 1, (kl, 128))
            else:
                brow[:, at] = select(mid_t, (k - nblk_o, e), each, mrows, 1, (kl, 128))
    scale = w_ref[:, pl.ds(pl.multiple_of(r * cq, 128), cq)] * (1.0 / nb_all)

    z_axis, row_axis = (Z, zi, z_dev), (R, r, row_dev)
    n = len(rest) // 3
    s1, s2, s3 = [
        Stream(rest[i * n:(i + 1) * n], blocks, z_first, core, pair_dev,
               (z_axis, row_axis) if z_first else (row_axis, z_axis))
        for i, (blocks, z_first) in enumerate(plan(nblk))]

    def arrive(k):
        for c in chunks[k]:
            c.wait()
        rows = slice(k * BLK, (k + 1) * BLK)
        v = x[rows, :].astype(F32) * scale
        h = v.astype(BF16)
        xw[k, :BLK, :] = h
        xw[k, BLK:, :] = (v - h.astype(F32)).astype(BF16)

    for stream in (s1, s2, s3):
        for k in stream.blocks:
            arrive(k)
        stream.compute(x, xw)
        stream.pair_start()
        if stream is s3:
            s1.two_start()
        stream.one_start()
    s1.back_start()
    s3.two_start()
    s2.two_start()
    s1.spread_rest()
    s3.back_start()
    s2.back_start()

    for c in id_copies:
        c.wait()
    owner = lax.div(b * kc, kl)
    begin = pl.multiple_of(lax.rem(b * kc, kl), 128)
    mid_c = ids[0, owner, :, pl.ds(begin, kc)]
    oid_c = ids[1, owner, :, pl.ds(begin, kc)]
    c_col = factors(ids[2, owner, :, pl.ds(begin, kc)], tt, entries)
    bcol = [select(oid_c, (k, 0), each, orows, 0, (BLK, kc)) for k in range(nblk_o)]
    bcol += [select(mid_c, (k, 0), each, mrows, 0, (BLK, kc)) for k in range(nblk_m)]

    t_o[...] = jnp.zeros_like(t_o)
    t_m[...] = jnp.zeros_like(t_m)
    cut = nblk_o * BLK

    def times(v, cols_of):
        total = None
        for p in split(v):
            total = dot(p, cols_of) if total is None else total + dot(p, cols_of)
        return total

    def gather(stream):
        stream.wait()
        at = 0
        for k in stream.blocks:
            m = (k + 1) * BLK
            strip = stream.full[at:at + m, :]
            at += m
            t = t_o if k < nblk_o else t_m
            t[:m, :] = t[:m, :] + times(strip, bcol[k])
            rows = slice(k * BLK, m)
            above = min(k * BLK, cut)
            if above > 0:
                part = jnp.concatenate(bcol[:above // BLK], axis=0)
                t_o[rows, :] = t_o[rows, :] + times(strip[:above, :].T, part)
            if k * BLK > cut:
                part = jnp.concatenate(bcol[nblk_o:k], axis=0)
                t_m[rows, :] = t_m[rows, :] + times(strip[cut:k * BLK, :].T, part)

    s1.pair_back()
    s3.spread_rest()
    s2.spread_rest()
    gather(s1)
    s3.pair_back()
    gather(s3)
    s2.pair_back()
    gather(s2)
    t = t_m[...] + t_o[...] * c_col
    g_o = times_left(brow[:, :cut], t[:cut, :])
    g_m = times_left(brow[:, cut:], t[cut:, :])
    gram_ref[...] = g_m + g_o * jnp.concatenate([c_row] * (kc // 128), axis=1)


def times_left(s, v):
    a, b = split(v)
    return dot(s, a) + dot(s, b)


def plan(nblk):
    half = nblk // 2
    return ((range(half), True), (range(half, nblk - 1), True), (range(nblk - 1, nblk), False))


def solution(mesh):
    R, B = mesh.shape["row"], mesh.shape["bus"]
    Z = B // 2

    def stream_scratch(blocks, n1, n2):
        unit = 8 * R * B
        packed = -(-(blocks * BLK) // unit) * unit
        H = packed // 2
        h1 = H // n1
        pz = h1 // n2
        dma = pltpu.SemaphoreType.DMA
        return [
            pltpu.VMEM((packed, BLK), F32),
            pltpu.VMEM((H, BLK), F32),
            pltpu.VMEM((H, BLK), F32),
            pltpu.VMEM((n1 - 1, h1, BLK), F32),
            pltpu.VMEM((h1, BLK), F32),
            pltpu.VMEM((n2 - 1, pz, BLK), F32),
            pltpu.VMEM((packed, BLK), F32),
            dma, dma,
            dma((n1 - 1,)), dma((n1 - 1,)),
            dma((n2 - 1,)), dma((n2 - 1,)),
            dma((Z - 1,)), dma((Z - 1,)),
            dma((Z, R - 1)), dma((Z, R - 1)),
            dma, dma,
        ]

    def local(monitored, outaged, bus_weight, lodf_table, mon_id, out_id, lodf_idx):
        mrows, cols = monitored.shape
        orows = outaged.shape[0]
        n = (mrows + orows) * R
        cq = cols // R
        nblk = n // BLK
        kl = mon_id.shape[0]
        kc = kl * R // B
        vmem = pl.BlockSpec(memory_space=pltpu.VMEM)
        hbm = pl.BlockSpec(memory_space=pl.ANY)
        dma = pltpu.SemaphoreType.DMA
        return pl.pallas_call(
            functools.partial(kernel, (R, B, cols * B)),
            out_shape=jax.ShapeDtypeStruct((kl, kc), F32),
            in_specs=[hbm] * 7,
            out_specs=vmem,
            scratch_shapes=[
                pltpu.VMEM((1, cols), F32),
                pltpu.VMEM((1, lodf_table.shape[0]), F32),
                pltpu.VMEM((1, kl), jnp.int32),
                pltpu.VMEM((1, kl), jnp.int32),
                pltpu.VMEM((1, kl), jnp.int32),
                dma((5,)),
                pltpu.VMEM((n, cq), BF16),
                pltpu.VMEM((nblk, 2 * BLK, cq), BF16),
                pltpu.VMEM((lodf_table.shape[0], 128), F32),
                pltpu.VMEM((3, R, 1, kl), jnp.int32),
                pltpu.VMEM((kl, n), BF16),
                pltpu.VMEM((n, kc), F32),
                pltpu.VMEM((n, kc), F32),
                dma((R - 1, nblk)), dma((R - 1, nblk)),
                dma((3, R - 1)), dma((3, R - 1)),
                dma((nblk,)), dma((3,)),
            ] + [
                ref for blocks, z_first in plan(nblk)
                for ref in stream_scratch(sum(k + 1 for k in blocks), *((Z, R) if z_first else (R, Z)))
            ],
            compiler_params=pltpu.CompilerParams(
                collective_id=0, has_side_effects=True, vmem_limit_bytes=60 * 1024 * 1024),
        )(monitored, outaged, bus_weight[None, :], lodf_table[None, :],
          mon_id[None, :], out_id[None, :], lodf_idx[None, :])

    in_specs = (P("row", "bus"), P("row", "bus"), P("bus"), P(), P("row"), P("row"), P("row"))
    return jax.shard_map(local, mesh=mesh, in_specs=in_specs, out_specs=P("row", "bus"), check_vma=False)
```

```python
import functools

import jax
import jax.numpy as jnp
from jax import lax
from jax.experimental import pallas as pl
from jax.experimental.pallas import tpu as pltpu
from jax.sharding import PartitionSpec as P

BLK = 128
F32 = jnp.float32
BF16 = jnp.bfloat16
MESH = pl.DeviceIdType.MESH


def split(v):
    a = v.astype(BF16)
    return a, (v - a.astype(F32)).astype(BF16)


def dot(a, b):
    return jnp.dot(a, b, preferred_element_type=F32)


def dot_t(a, b):
    return lax.dot_general(a, b, (((1,), (1,)), ((), ())), preferred_element_type=F32)


def down(lanes):
    n = lanes.shape[1]
    return jnp.broadcast_to(lanes, (128, n)).T


def factors(idx, table_t, entries):
    n = idx.shape[1]
    parts = []
    for lo in range(0, n, 128):
        total = jnp.zeros((1, 128), F32)
        for e in range(0, entries, 128):
            rows = lax.broadcasted_iota(jnp.int32, (128, 128), 0) + e
            hit = jnp.where(rows == idx[:, lo:lo + 128], table_t[e:e + 128, :], 0.0)
            total = total + jnp.sum(hit, axis=0, keepdims=True)
        parts.append(total)
    return jnp.concatenate(parts, axis=1)


class Stream:
    def __init__(self, refs, blocks, z_first, z_back, core, other, axes):
        (self.gp, self.cbuf, self.acc, self.b1, self.s1, self.b2, self.full,
         self.cs, self.cr, self.p1s, self.p1r, self.p2s, self.p2r,
         self.a1s, self.a1r, self.a2s, self.a2r, self.ds, self.dr) = refs
        self.blocks = blocks
        self.core, self.other = core, other
        (self.n1, self.i1, self.dev1), (self.n2, self.i2, self.dev2) = axes
        self.H = self.gp.shape[0] // 2
        self.h1 = self.H // self.n1
        self.pz = self.h1 // self.n2
        self.z_first, self.z_back = z_first, z_back

    def compute(self, x, xw):
        at = 0
        for k in self.blocks:
            m = (k + 1) * BLK
            both = dot_t(x[:m, :], xw[k])
            self.gp[at:at + m, :] = both[:, :BLK] + both[:, BLK:]
            at += m
        if self.gp.shape[0] > at:
            self.gp[at:, :] = jnp.zeros((self.gp.shape[0] - at, BLK), F32)

    def rows(self, start, count):
        return pl.ds(pl.multiple_of(start, 8), count)

    def send(self, src, dst, s, r, dev):
        c = pltpu.make_async_remote_copy(
            src_ref=src, dst_ref=dst, send_sem=s, recv_sem=r, device_id=dev, device_id_type=MESH)
        c.start()
        return c

    def pair_start(self):
        self.c = [self.send(self.gp.at[self.rows((1 - self.core) * self.H, self.H), :], self.cbuf,
                            self.cs, self.cr, self.other)]

    def wait(self):
        for c in self.c:
            c.wait()

    def one_start(self):
        self.wait()
        self.acc[...] = self.gp[self.rows(self.core * self.H, self.H), :] + self.cbuf[...]
        self.c = []
        for d in range(1, self.n1):
            q = lax.rem(self.i1 + d, self.n1)
            self.c.append(self.send(self.acc.at[self.rows(q * self.h1, self.h1), :], self.b1.at[d - 1],
                                    self.p1s.at[d - 1], self.p1r.at[d - 1], self.dev1(q)))

    def two_start(self):
        self.wait()
        total = self.acc[self.rows(self.i1 * self.h1, self.h1), :]
        for d in range(1, self.n1):
            total = total + self.b1[d - 1]
        self.s1[...] = total
        self.c = []
        for d in range(1, self.n2):
            q = lax.rem(self.i2 + d, self.n2)
            self.c.append(self.send(self.s1.at[self.rows(q * self.pz, self.pz), :], self.b2.at[d - 1],
                                    self.p2s.at[d - 1], self.p2r.at[d - 1], self.dev2(q)))

    def piece(self, z, r):
        i1, i2 = (z, r) if self.z_first else (r, z)
        return self.rows(self.core * self.H + i1 * self.h1 + i2 * self.pz, self.pz)

    def back_start(self):
        self.wait()
        total = self.s1[self.rows(self.i2 * self.pz, self.pz), :]
        for d in range(1, self.n2):
            total = total + self.b2[d - 1]
        one, two = (self.n1, self.i1, self.dev1), (self.n2, self.i2, self.dev2)
        if self.z_first != self.z_back:
            one, two = two, one
        (self.m1, self.k1, self.to1), (self.m2, self.k2, self.to2) = one, two
        at = self.back_piece(self.k1)
        self.full[at, :] = total
        ref = self.full.at[at, :]
        self.zc = []
        for d in range(1, self.m1):
            self.zc.append(self.send(ref, ref, self.a1s.at[d - 1], self.a1r.at[d - 1],
                                     self.to1(lax.rem(self.k1 + d, self.m1))))
        self.c = []
        self.spread(0)

    def back_piece(self, k):
        return self.piece(k, self.k2) if self.z_back else self.piece(self.k2, k)

    def spread(self, e):
        ref = self.full.at[self.back_piece(lax.rem(self.k1 + self.m1 - e, self.m1)), :]
        for d in range(1, self.m2):
            self.c.append(self.send(ref, ref, self.a2s.at[e, d - 1], self.a2r.at[e, d - 1],
                                    self.to2(lax.rem(self.k2 + d, self.m2))))

    def spread_rest(self):
        for e in range(1, self.m1):
            self.zc[e - 1].wait()
            self.spread(e)

    def pair_back(self):
        self.wait()
        ref = self.full.at[self.rows(self.core * self.H, self.H), :]
        self.c = [self.send(ref, ref, self.ds, self.dr, self.other)]


def select(ids, block, rows_each, dev_rows, axis, shape):
    p = lax.broadcasted_iota(jnp.int32, shape, axis)
    if axis == 1:
        p = p + block[1]
    shift = rows_each.bit_length() - 1
    line = lax.shift_right_logical(p, jnp.full(shape, shift, jnp.int32)) * (dev_rows - rows_each) + p
    return jnp.where(ids == line + block[0] * rows_each, 1.0, 0.0).astype(BF16)


def kernel(dims, mon_ref, out_ref, w_hbm, table_hbm, mid_hbm, oid_hbm, lid_hbm,
           gram_ref, w_ref, table_ref, mid_ref, oid_ref, lid_ref, small, x, xw, tt, ids, brow, t_o, t_m, x_s, x_r, i_s, i_r, own, own_i, *rest):
    R, B, nb_all = dims
    Z = B // 2
    r = lax.axis_index("row")
    b = lax.axis_index("bus")
    core = lax.rem(b, 2)
    zi = lax.div(b, 2)
    mrows, cols = mon_ref.shape
    orows = out_ref.shape[0]
    each = BLK // R
    cq = cols // R
    nblk_o, nblk_m = orows // each, mrows // each
    nblk = nblk_m + nblk_o
    kl = mid_ref.shape[1]
    kc = kl * R // B
    loads = []
    for i, (src, dst) in enumerate(((w_hbm, w_ref), (table_hbm, table_ref), (mid_hbm, mid_ref),
                                    (oid_hbm, oid_ref), (lid_hbm, lid_ref))):
        c = pltpu.make_async_copy(src, dst, small.at[i])
        c.start()
        loads.append(c)

    def row_dev(q):
        return {"row": q}

    def z_dev(q):
        return {"bus": q * 2 + core}

    pair_dev = {"bus": zi * 2 + (1 - core)}
    barrier = pltpu.get_barrier_semaphore()
    for d in range(1, R):
        pl.semaphore_signal(barrier, inc=1, device_id=row_dev(lax.rem(r + d, R)), device_id_type=MESH)
    for d in range(1, Z):
        pl.semaphore_signal(barrier, inc=1, device_id=z_dev(lax.rem(zi + d, Z)), device_id_type=MESH)
    pl.semaphore_signal(barrier, inc=1, device_id=pair_dev, device_id_type=MESH)
    pl.semaphore_wait(barrier, R - 1 + Z - 1 + 1)

    def source(k, q):
        ref, k = (out_ref, k) if k < nblk_o else (mon_ref, k - nblk_o)
        return ref.at[k * each:(k + 1) * each, pl.ds(pl.multiple_of(q * cq, 128), cq)]

    def target(k):
        return x.at[pl.ds(pl.multiple_of(k * BLK + r * each, each), each), :]

    chunks = []
    for k in range(nblk):
        chunk = []
        for d in range(1, R):
            q = lax.rem(r + d, R)
            c = pltpu.make_async_remote_copy(
                src_ref=source(k, q), dst_ref=target(k), send_sem=x_s.at[d - 1, k], recv_sem=x_r.at[d - 1, k],
                device_id=row_dev(q), device_id_type=MESH)
            c.start()
            chunk.append(c)
        c = pltpu.make_async_copy(source(k, r), target(k), own.at[k])
        c.start()
        chunk.append(c)
        chunks.append(chunk)
    for c in loads:
        c.wait()
    id_copies = []
    for i, src in enumerate((mid_ref, oid_ref, lid_ref)):
        for d in range(1, R):
            c = pltpu.make_async_remote_copy(
                src_ref=src, dst_ref=ids.at[i, r], send_sem=i_s.at[i, d - 1], recv_sem=i_r.at[i, d - 1],
                device_id=row_dev(lax.rem(r + d, R)), device_id_type=MESH)
            c.start()
            id_copies.append(c)
        c = pltpu.make_async_copy(src, ids.at[i, r], own_i.at[i])
        c.start()
        id_copies.append(c)

    entries = table_ref.shape[1]
    for e in range(0, entries, 128):
        tt[e:e + 128, :] = down(table_ref[:, e:e + 128])
    c_row = down(factors(lid_ref[...], tt, entries))
    oid_t = down(oid_ref[...].astype(F32)).astype(jnp.int32)
    mid_t = down(mid_ref[...].astype(F32)).astype(jnp.int32)
    for k in range(nblk):
        for e in range(0, BLK, 128):
            at = slice(k * BLK + e, k * BLK + e + 128)
            if k < nblk_o:
                brow[:, at] = select(oid_t, (k, e), each, orows, 1, (kl, 128))
            else:
                brow[:, at] = select(mid_t, (k - nblk_o, e), each, mrows, 1, (kl, 128))
    scale = w_ref[:, pl.ds(pl.multiple_of(r * cq, 128), cq)] * (1.0 / nb_all)

    z_axis, row_axis = (Z, zi, z_dev), (R, r, row_dev)
    n = len(rest) // 3
    s1, s2, s3 = [
        Stream(rest[i * n:(i + 1) * n], blocks, z_first, z_back, core, pair_dev,
               (z_axis, row_axis) if z_first else (row_axis, z_axis))
        for i, (blocks, z_first, z_back) in enumerate(plan(nblk))]

    def arrive(k):
        for c in chunks[k]:
            c.wait()
        rows = slice(k * BLK, (k + 1) * BLK)
        v = x[rows, :].astype(F32) * scale
        h = v.astype(BF16)
        xw[k, :BLK, :] = h
        xw[k, BLK:, :] = (v - h.astype(F32)).astype(BF16)

    for stream in (s1, s2, s3):
        for k in stream.blocks:
            arrive(k)
        stream.compute(x, xw)
        stream.pair_start()
        if stream is s3:
            s1.two_start()
        stream.one_start()
    s1.back_start()
    s3.two_start()
    s2.two_start()
    s1.spread_rest()
    s3.back_start()
    s2.back_start()

    for c in id_copies:
        c.wait()
    owner = lax.div(b * kc, kl)
    begin = pl.multiple_of(lax.rem(b * kc, kl), 128)
    mid_c = ids[0, owner, :, pl.ds(begin, kc)]
    oid_c = ids[1, owner, :, pl.ds(begin, kc)]
    c_col = factors(ids[2, owner, :, pl.ds(begin, kc)], tt, entries)
    bcol = [select(oid_c, (k, 0), each, orows, 0, (BLK, kc)) for k in range(nblk_o)]
    bcol += [select(mid_c, (k, 0), each, mrows, 0, (BLK, kc)) for k in range(nblk_m)]

    t_o[...] = jnp.zeros_like(t_o)
    t_m[...] = jnp.zeros_like(t_m)
    cut = nblk_o * BLK

    def times(v, cols_of):
        total = None
        for p in split(v):
            total = dot(p, cols_of) if total is None else total + dot(p, cols_of)
        return total

    def gather(stream):
        stream.wait()
        at = 0
        for k in stream.blocks:
            m = (k + 1) * BLK
            strip = stream.full[at:at + m, :]
            at += m
            t = t_o if k < nblk_o else t_m
            t[:m, :] = t[:m, :] + times(strip, bcol[k])
            rows = slice(k * BLK, m)
            above = min(k * BLK, cut)
            if above > 0:
                part = jnp.concatenate(bcol[:above // BLK], axis=0)
                t_o[rows, :] = t_o[rows, :] + times(strip[:above, :].T, part)
            if k * BLK > cut:
                part = jnp.concatenate(bcol[nblk_o:k], axis=0)
                t_m[rows, :] = t_m[rows, :] + times(strip[cut:k * BLK, :].T, part)

    s3.spread_rest()
    s2.spread_rest()
    s1.pair_back()
    s3.pair_back()
    gather(s1)
    s2.pair_back()
    gather(s3)
    gather(s2)
    t = t_m[...] + t_o[...] * c_col
    g_o = times_left(brow[:, :cut], t[:cut, :])
    g_m = times_left(brow[:, cut:], t[cut:, :])
    gram_ref[...] = g_m + g_o * jnp.concatenate([c_row] * (kc // 128), axis=1)


def times_left(s, v):
    a, b = split(v)
    return dot(s, a) + dot(s, b)


def plan(nblk):
    half = nblk // 2
    return ((range(half), True, False), (range(half, nblk - 1), True, True),
            (range(nblk - 1, nblk), False, True))


def solution(mesh):
    R, B = mesh.shape["row"], mesh.shape["bus"]
    Z = B // 2

    def stream_scratch(blocks, n1, n2, m1, m2):
        unit = 8 * R * B
        packed = -(-(blocks * BLK) // unit) * unit
        H = packed // 2
        h1 = H // n1
        pz = h1 // n2
        dma = pltpu.SemaphoreType.DMA
        return [
            pltpu.VMEM((packed, BLK), F32),
            pltpu.VMEM((H, BLK), F32),
            pltpu.VMEM((H, BLK), F32),
            pltpu.VMEM((n1 - 1, h1, BLK), F32),
            pltpu.VMEM((h1, BLK), F32),
            pltpu.VMEM((n2 - 1, pz, BLK), F32),
            pltpu.VMEM((packed, BLK), F32),
            dma, dma,
            dma((n1 - 1,)), dma((n1 - 1,)),
            dma((n2 - 1,)), dma((n2 - 1,)),
            dma((m1 - 1,)), dma((m1 - 1,)),
            dma((m1, m2 - 1)), dma((m1, m2 - 1)),
            dma, dma,
        ]

    def local(monitored, outaged, bus_weight, lodf_table, mon_id, out_id, lodf_idx):
        mrows, cols = monitored.shape
        orows = outaged.shape[0]
        n = (mrows + orows) * R
        cq = cols // R
        nblk = n // BLK
        kl = mon_id.shape[0]
        kc = kl * R // B
        vmem = pl.BlockSpec(memory_space=pltpu.VMEM)
        hbm = pl.BlockSpec(memory_space=pl.ANY)
        dma = pltpu.SemaphoreType.DMA
        return pl.pallas_call(
            functools.partial(kernel, (R, B, cols * B)),
            out_shape=jax.ShapeDtypeStruct((kl, kc), F32),
            in_specs=[hbm] * 7,
            out_specs=vmem,
            scratch_shapes=[
                pltpu.VMEM((1, cols), F32),
                pltpu.VMEM((1, lodf_table.shape[0]), F32),
                pltpu.VMEM((1, kl), jnp.int32),
                pltpu.VMEM((1, kl), jnp.int32),
                pltpu.VMEM((1, kl), jnp.int32),
                dma((5,)),
                pltpu.VMEM((n, cq), BF16),
                pltpu.VMEM((nblk, 2 * BLK, cq), BF16),
                pltpu.VMEM((lodf_table.shape[0], 128), F32),
                pltpu.VMEM((3, R, 1, kl), jnp.int32),
                pltpu.VMEM((kl, n), BF16),
                pltpu.VMEM((n, kc), F32),
                pltpu.VMEM((n, kc), F32),
                dma((R - 1, nblk)), dma((R - 1, nblk)),
                dma((3, R - 1)), dma((3, R - 1)),
                dma((nblk,)), dma((3,)),
            ] + [
                ref for blocks, z_first, z_back in plan(nblk)
                for ref in stream_scratch(sum(k + 1 for k in blocks), *((Z, R) if z_first else (R, Z)),
                                          *((Z, R) if z_back else (R, Z)))
            ],
            compiler_params=pltpu.CompilerParams(
                collective_id=0, has_side_effects=True, vmem_limit_bytes=60 * 1024 * 1024),
        )(monitored, outaged, bus_weight[None, :], lodf_table[None, :],
          mon_id[None, :], out_id[None, :], lodf_idx[None, :])

    in_specs = (P("row", "bus"), P("row", "bus"), P("bus"), P(), P("row"), P("row"), P("row"))
    return jax.shard_map(local, mesh=mesh, in_specs=in_specs, out_specs=P("row", "bus"), check_vma=False)
```

```python
import functools

import jax
import jax.numpy as jnp
from jax import lax
from jax.experimental import pallas as pl
from jax.experimental.pallas import tpu as pltpu
from jax.sharding import PartitionSpec as P

BLK = 128
F32 = jnp.float32
BF16 = jnp.bfloat16
MESH = pl.DeviceIdType.MESH


def split(v):
    a = v.astype(BF16)
    return a, (v - a.astype(F32)).astype(BF16)


def dot(a, b):
    return jnp.dot(a, b, preferred_element_type=F32)


def dot_t(a, b):
    return lax.dot_general(a, b, (((1,), (1,)), ((), ())), preferred_element_type=F32)


def down(lanes):
    n = lanes.shape[1]
    return jnp.broadcast_to(lanes, (128, n)).T


def factors(idx, table_t, entries):
    n = idx.shape[1]
    parts = []
    for lo in range(0, n, 128):
        total = jnp.zeros((1, 128), F32)
        for e in range(0, entries, 128):
            rows = lax.broadcasted_iota(jnp.int32, (128, 128), 0) + e
            hit = jnp.where(rows == idx[:, lo:lo + 128], table_t[e:e + 128, :], 0.0)
            total = total + jnp.sum(hit, axis=0, keepdims=True)
        parts.append(total)
    return jnp.concatenate(parts, axis=1)


class Stream:
    def __init__(self, refs, blocks, me, core, other, axes):
        (self.gp, self.cbuf, self.acc, self.b1, self.s1, self.b2, self.full,
         self.cs, self.cr, self.p1s, self.p1r, self.p2s, self.p2r,
         self.a1s, self.a1r, self.a2s, self.a2r, self.ds, self.dr) = refs
        self.blocks = blocks
        self.core, self.other = core, other
        (self.n1, self.i1, self.dev1), (self.n2, self.i2, self.dev2) = axes
        self.H = self.gp.shape[0] // 2
        self.h1 = self.H // self.n1
        self.pz = self.h1 // self.n2
        self.z_first = me

    def compute(self, x, xw):
        at = 0
        for k in self.blocks:
            m = (k + 1) * BLK
            both = dot_t(x[:m, :], xw[k])
            self.gp[at:at + m, :] = both[:, :BLK] + both[:, BLK:]
            at += m
        if self.gp.shape[0] > at:
            self.gp[at:, :] = jnp.zeros((self.gp.shape[0] - at, BLK), F32)

    def rows(self, start, count):
        return pl.ds(pl.multiple_of(start, 8), count)

    def send(self, src, dst, s, r, dev):
        c = pltpu.make_async_remote_copy(
            src_ref=src, dst_ref=dst, send_sem=s, recv_sem=r, device_id=dev, device_id_type=MESH)
        c.start()
        return c

    def pair_start(self):
        self.c = [self.send(self.gp.at[self.rows((1 - self.core) * self.H, self.H), :], self.cbuf,
                            self.cs, self.cr, self.other)]

    def wait(self):
        for c in self.c:
            c.wait()

    def one_start(self):
        self.wait()
        self.acc[...] = self.gp[self.rows(self.core * self.H, self.H), :] + self.cbuf[...]
        self.c = []
        for d in range(1, self.n1):
            q = lax.rem(self.i1 + d, self.n1)
            self.c.append(self.send(self.acc.at[self.rows(q * self.h1, self.h1), :], self.b1.at[d - 1],
                                    self.p1s.at[d - 1], self.p1r.at[d - 1], self.dev1(q)))

    def two_start(self):
        self.wait()
        total = self.acc[self.rows(self.i1 * self.h1, self.h1), :]
        for d in range(1, self.n1):
            total = total + self.b1[d - 1]
        self.s1[...] = total
        self.c = []
        for d in range(1, self.n2):
            q = lax.rem(self.i2 + d, self.n2)
            self.c.append(self.send(self.s1.at[self.rows(q * self.pz, self.pz), :], self.b2.at[d - 1],
                                    self.p2s.at[d - 1], self.p2r.at[d - 1], self.dev2(q)))

    def piece(self, z, r):
        i1, i2 = (z, r) if self.z_first else (r, z)
        return self.rows(self.core * self.H + i1 * self.h1 + i2 * self.pz, self.pz)

    def back_start(self):
        self.wait()
        total = self.s1[self.rows(self.i2 * self.pz, self.pz), :]
        for d in range(1, self.n2):
            total = total + self.b2[d - 1]
        if self.z_first:
            self.Z, self.zi, self.zdev = self.n1, self.i1, self.dev1
            self.R, self.r, self.rdev = self.n2, self.i2, self.dev2
        else:
            self.Z, self.zi, self.zdev = self.n2, self.i2, self.dev2
            self.R, self.r, self.rdev = self.n1, self.i1, self.dev1
        at = self.piece(self.zi, self.r)
        self.full[at, :] = total
        ref = self.full.at[at, :]
        self.zc = []
        for d in range(1, self.Z):
            self.zc.append(self.send(ref, ref, self.a1s.at[d - 1], self.a1r.at[d - 1],
                                     self.zdev(lax.rem(self.zi + d, self.Z))))
        self.c = []
        self.spread(0)

    def spread(self, e):
        ref = self.full.at[self.piece(lax.rem(self.zi + self.Z - e, self.Z), self.r), :]
        for d in range(1, self.R):
            self.c.append(self.send(ref, ref, self.a2s.at[e, d - 1], self.a2r.at[e, d - 1],
                                    self.rdev(lax.rem(self.r + d, self.R))))

    def spread_rest(self):
        for e in range(1, self.Z):
            self.zc[e - 1].wait()
            self.spread(e)

    def pair_back(self):
        self.wait()
        ref = self.full.at[self.rows(self.core * self.H, self.H), :]
        self.c = [self.send(ref, ref, self.ds, self.dr, self.other)]


def select(ids, block, rows_each, dev_rows, axis, shape):
    p = lax.broadcasted_iota(jnp.int32, shape, axis)
    if axis == 1:
        p = p + block[1]
    shift = rows_each.bit_length() - 1
    line = lax.shift_right_logical(p, jnp.full(shape, shift, jnp.int32)) * (dev_rows - rows_each) + p
    return jnp.where(ids == line + block[0] * rows_each, 1.0, 0.0).astype(BF16)


def kernel(dims, mon_ref, out_ref, w_hbm, table_hbm, mid_hbm, oid_hbm, lid_hbm,
           gram_ref, w_ref, table_ref, mid_ref, oid_ref, lid_ref, small, x, xw, tt, ids, brow, t_o, t_m, x_s, x_r, i_s, i_r, own, own_i, *rest):
    R, B, nb_all = dims
    Z = B // 2
    r = lax.axis_index("row")
    b = lax.axis_index("bus")
    core = lax.rem(b, 2)
    zi = lax.div(b, 2)
    mrows, cols = mon_ref.shape
    orows = out_ref.shape[0]
    each = BLK // R
    cq = cols // R
    nblk_o, nblk_m = orows // each, mrows // each
    nblk = nblk_m + nblk_o
    kl = mid_ref.shape[1]
    kc = kl * R // B
    loads = []
    for i, (src, dst) in enumerate(((w_hbm, w_ref), (table_hbm, table_ref), (mid_hbm, mid_ref),
                                    (oid_hbm, oid_ref), (lid_hbm, lid_ref))):
        c = pltpu.make_async_copy(src, dst, small.at[i])
        c.start()
        loads.append(c)

    def row_dev(q):
        return {"row": q}

    def z_dev(q):
        return {"bus": q * 2 + core}

    pair_dev = {"bus": zi * 2 + (1 - core)}
    barrier = pltpu.get_barrier_semaphore()
    for d in range(1, R):
        pl.semaphore_signal(barrier, inc=1, device_id=row_dev(lax.rem(r + d, R)), device_id_type=MESH)
    for d in range(1, Z):
        pl.semaphore_signal(barrier, inc=1, device_id=z_dev(lax.rem(zi + d, Z)), device_id_type=MESH)
    pl.semaphore_signal(barrier, inc=1, device_id=pair_dev, device_id_type=MESH)
    pl.semaphore_wait(barrier, R - 1 + Z - 1 + 1)

    def source(k, q):
        ref, k = (out_ref, k) if k < nblk_o else (mon_ref, k - nblk_o)
        return ref.at[k * each:(k + 1) * each, pl.ds(pl.multiple_of(q * cq, 128), cq)]

    def target(k):
        return x.at[pl.ds(pl.multiple_of(k * BLK + r * each, each), each), :]

    chunks = []
    for k in range(nblk):
        chunk = []
        for d in range(1, R):
            q = lax.rem(r + d, R)
            c = pltpu.make_async_remote_copy(
                src_ref=source(k, q), dst_ref=target(k), send_sem=x_s.at[d - 1, k], recv_sem=x_r.at[d - 1, k],
                device_id=row_dev(q), device_id_type=MESH)
            c.start()
            chunk.append(c)
        c = pltpu.make_async_copy(source(k, r), target(k), own.at[k])
        c.start()
        chunk.append(c)
        chunks.append(chunk)
    for c in loads:
        c.wait()
    id_copies = []
    for i, src in enumerate((mid_ref, oid_ref, lid_ref)):
        for d in range(1, R):
            c = pltpu.make_async_remote_copy(
                src_ref=src, dst_ref=ids.at[i, r], send_sem=i_s.at[i, d - 1], recv_sem=i_r.at[i, d - 1],
                device_id=row_dev(lax.rem(r + d, R)), device_id_type=MESH)
            c.start()
            id_copies.append(c)
        c = pltpu.make_async_copy(src, ids.at[i, r], own_i.at[i])
        c.start()
        id_copies.append(c)

    entries = table_ref.shape[1]
    for e in range(0, entries, 128):
        tt[e:e + 128, :] = down(table_ref[:, e:e + 128])
    c_row = down(factors(lid_ref[...], tt, entries))
    oid_t = down(oid_ref[...].astype(F32)).astype(jnp.int32)
    mid_t = down(mid_ref[...].astype(F32)).astype(jnp.int32)
    for k in range(nblk):
        for e in range(0, BLK, 128):
            at = slice(k * BLK + e, k * BLK + e + 128)
            if k < nblk_o:
                brow[:, at] = select(oid_t, (k, e), each, orows, 1, (kl, 128))
            else:
                brow[:, at] = select(mid_t, (k - nblk_o, e), each, mrows, 1, (kl, 128))
    scale = w_ref[:, pl.ds(pl.multiple_of(r * cq, 128), cq)] * (1.0 / nb_all)

    z_axis, row_axis = (Z, zi, z_dev), (R, r, row_dev)
    n = len(rest) // 2
    s1, s2 = [
        Stream(rest[i * n:(i + 1) * n], blocks, z_first, core, pair_dev,
               (z_axis, row_axis) if z_first else (row_axis, z_axis))
        for i, (blocks, z_first) in enumerate(plan(nblk))]

    def arrive(k):
        for c in chunks[k]:
            c.wait()
        rows = slice(k * BLK, (k + 1) * BLK)
        v = x[rows, :].astype(F32) * scale
        h = v.astype(BF16)
        xw[k, :BLK, :] = h
        xw[k, BLK:, :] = (v - h.astype(F32)).astype(BF16)

    for stream in (s1, s2):
        for k in stream.blocks:
            arrive(k)
        stream.compute(x, xw)
        stream.pair_start()
        stream.one_start()
    s1.two_start()
    s2.two_start()
    s1.back_start()
    s2.back_start()
    s1.spread_rest()

    for c in id_copies:
        c.wait()
    owner = lax.div(b * kc, kl)
    begin = pl.multiple_of(lax.rem(b * kc, kl), 128)
    mid_c = ids[0, owner, :, pl.ds(begin, kc)]
    oid_c = ids[1, owner, :, pl.ds(begin, kc)]
    c_col = factors(ids[2, owner, :, pl.ds(begin, kc)], tt, entries)
    bcol = [select(oid_c, (k, 0), each, orows, 0, (BLK, kc)) for k in range(nblk_o)]
    bcol += [select(mid_c, (k, 0), each, mrows, 0, (BLK, kc)) for k in range(nblk_m)]

    t_o[...] = jnp.zeros_like(t_o)
    t_m[...] = jnp.zeros_like(t_m)
    cut = nblk_o * BLK

    def times(v, cols_of):
        total = None
        for p in split(v):
            total = dot(p, cols_of) if total is None else total + dot(p, cols_of)
        return total

    def gather(stream):
        stream.wait()
        at = 0
        for k in stream.blocks:
            m = (k + 1) * BLK
            strip = stream.full[at:at + m, :]
            at += m
            t = t_o if k < nblk_o else t_m
            t[:m, :] = t[:m, :] + times(strip, bcol[k])
            rows = slice(k * BLK, m)
            above = min(k * BLK, cut)
            if above > 0:
                part = jnp.concatenate(bcol[:above // BLK], axis=0)
                t_o[rows, :] = t_o[rows, :] + times(strip[:above, :].T, part)
            if k * BLK > cut:
                part = jnp.concatenate(bcol[nblk_o:k], axis=0)
                t_m[rows, :] = t_m[rows, :] + times(strip[cut:k * BLK, :].T, part)

    s2.spread_rest()
    s1.pair_back()
    gather(s1)
    s2.pair_back()
    gather(s2)
    t = t_m[...] + t_o[...] * c_col
    g_o = times_left(brow[:, :cut], t[:cut, :])
    g_m = times_left(brow[:, cut:], t[cut:, :])
    gram_ref[...] = g_m + g_o * jnp.concatenate([c_row] * (kc // 128), axis=1)


def times_left(s, v):
    a, b = split(v)
    return dot(s, a) + dot(s, b)


def plan(nblk):
    early = nblk - nblk // 3
    return (range(early), True), (range(early, nblk), False)


def solution(mesh):
    R, B = mesh.shape["row"], mesh.shape["bus"]
    Z = B // 2

    def stream_scratch(blocks, n1, n2):
        unit = 8 * R * B
        packed = -(-(blocks * BLK) // unit) * unit
        H = packed // 2
        h1 = H // n1
        pz = h1 // n2
        dma = pltpu.SemaphoreType.DMA
        return [
            pltpu.VMEM((packed, BLK), F32),
            pltpu.VMEM((H, BLK), F32),
            pltpu.VMEM((H, BLK), F32),
            pltpu.VMEM((n1 - 1, h1, BLK), F32),
            pltpu.VMEM((h1, BLK), F32),
            pltpu.VMEM((n2 - 1, pz, BLK), F32),
            pltpu.VMEM((packed, BLK), F32),
            dma, dma,
            dma((n1 - 1,)), dma((n1 - 1,)),
            dma((n2 - 1,)), dma((n2 - 1,)),
            dma((Z - 1,)), dma((Z - 1,)),
            dma((Z, R - 1)), dma((Z, R - 1)),
            dma, dma,
        ]

    def local(monitored, outaged, bus_weight, lodf_table, mon_id, out_id, lodf_idx):
        mrows, cols = monitored.shape
        orows = outaged.shape[0]
        n = (mrows + orows) * R
        cq = cols // R
        nblk = n // BLK
        kl = mon_id.shape[0]
        kc = kl * R // B
        vmem = pl.BlockSpec(memory_space=pltpu.VMEM)
        hbm = pl.BlockSpec(memory_space=pl.ANY)
        dma = pltpu.SemaphoreType.DMA
        return pl.pallas_call(
            functools.partial(kernel, (R, B, cols * B)),
            out_shape=jax.ShapeDtypeStruct((kl, kc), F32),
            in_specs=[hbm] * 7,
            out_specs=vmem,
            scratch_shapes=[
                pltpu.VMEM((1, cols), F32),
                pltpu.VMEM((1, lodf_table.shape[0]), F32),
                pltpu.VMEM((1, kl), jnp.int32),
                pltpu.VMEM((1, kl), jnp.int32),
                pltpu.VMEM((1, kl), jnp.int32),
                dma((5,)),
                pltpu.VMEM((n, cq), BF16),
                pltpu.VMEM((nblk, 2 * BLK, cq), BF16),
                pltpu.VMEM((lodf_table.shape[0], 128), F32),
                pltpu.VMEM((3, R, 1, kl), jnp.int32),
                pltpu.VMEM((kl, n), BF16),
                pltpu.VMEM((n, kc), F32),
                pltpu.VMEM((n, kc), F32),
                dma((R - 1, nblk)), dma((R - 1, nblk)),
                dma((3, R - 1)), dma((3, R - 1)),
                dma((nblk,)), dma((3,)),
            ] + [
                ref for blocks, z_first in plan(nblk)
                for ref in stream_scratch(sum(k + 1 for k in blocks), *((Z, R) if z_first else (R, Z)))
            ],
            compiler_params=pltpu.CompilerParams(
                collective_id=0, has_side_effects=True, vmem_limit_bytes=60 * 1024 * 1024),
        )(monitored, outaged, bus_weight[None, :], lodf_table[None, :],
          mon_id[None, :], out_id[None, :], lodf_idx[None, :])

    in_specs = (P("row", "bus"), P("row", "bus"), P("bus"), P(), P("row"), P("row"), P("row"))
    return jax.shard_map(local, mesh=mesh, in_specs=in_specs, out_specs=P("row", "bus"), check_vma=False)
```
